32 devices in a mesh: groups: 2 (over y), req: 2 (over x), head: 4 (over z), sec: 2 (over core).
Axes of the slice: x: 2, y: 2, z: 4, core: 2. Of those that a mesh axis runs over, the one named last changes fastest.
Arguments:
- queries: bfloat16 [512, 4096], P(('groups', 'req'), ('head', 'sec')), parts along dimension 0, may hold values from -16 to 16
- cache_pool: bfloat16 [48, 128, 8, 128], P(('groups', 'req'), None, 'head'), parts along dimension 0, may hold values from -4 to 4
- lengths: int32 [4], P(('groups', 'req')), parts along dimension 0, may hold values from 128 to 1536, as said below
- block_table: int32 [4, 12], P(('groups', 'req')), parts along dimension 0, may hold values from 0 to 11, as said below
- out_proj: bfloat16 [4096, 2880], P(('head', 'sec')), may hold values from -0.375 to 0.375
- residual_in: bfloat16 [512, 2880], P(('groups', 'req', 'head', 'sec')), parts along dimension 0, may hold values from -16 to 16
- norm_gain: float32 [2880], replicated, may hold values from 0.1 to 1.9
- expert_ids: int32 [512, 4], P(('groups', 'req', 'head', 'sec')), parts along dimension 0, may hold values from 0 to 7, all different within a row; in each aligned block of 16 rows (0 to 15, 16 to 31, ...) at most 8 rows name the same one
- route_weight: float32 [512, 4], P(('groups', 'req', 'head', 'sec')), parts along dimension 0, may hold values from 0.2 to 1
- gate_weight: bfloat16 [8, 2880, 2880], P(('head', 'sec'), None, 'req'), may hold values from -0.109375 to 0.109375
- up_weight: bfloat16 [8, 2880, 2880], P(('head', 'sec'), None, 'req'), may hold values from -0.109375 to 0.109375
- down_weight: bfloat16 [8, 2880, 2880], P(('head', 'sec'), 'req'), may hold values from -0.109375 to 0.109375
Outputs:
- layer_out: bfloat16 [512, 2880], P(('groups', 'req', 'head', 'sec')), parts along dimension 0
The draws below stay inside these ranges and needn't reach their ends.
There are 2 independent parts, one for each index of `groups`. The reference program is written for one: setup_inputs(seed, part) draws one part's arguments, and reference() takes and returns one part's arrays. A program takes and returns all parts, laid end to end along the dimension named above; an argument that names none is the same for every part. Nothing has to cross between parts.
Inputs may be any that keep to these rules, and one draw needn't show every extreme that they name: lengths[r] counts request r's positions, its last 128 positions being its new rows; some request reaches 1536 in every draw. `block_table`: each row is a permutation of 0 to 11. `expert_ids`: a row names 4 different experts; in each aligned block of 16 rows every expert is named by exactly 8 rows.
All inputs are finite; a program needn't handle non-finite values.
Results may differ from the reference program's by a relative error of at most 0.017.
Values may be sent and summed in bfloat16 or wider, within the bound.
A program may use at most 128 MiB of HBM per device.

```python
import math
import jax
import jax.numpy as jnp
import numpy as np
from jax import lax

D = 2880
QH = 64
KVH = 8
HD = 64
HID = 2880
TOP = 4
BLK = 128
MAXB = 12
NEW = 128
REQS = 2
ROWS = 256
QGROUPS = 8
HSHARDS = 2
EXPERTS = 8
ROWS_DEV = 16
CAP = 8


def draw_queries(key, part):
    gaussian = jax.random.normal(jax.random.fold_in(key, 21), (ROWS, QH, HD), jnp.float32)
    values = 2.0 * gaussian
    return jnp.clip(values, -16.0, 16.0).reshape(ROWS, QH * HD).astype(jnp.bfloat16)


def draw_cache_pool(key, part):
    gaussian = jax.random.normal(jax.random.fold_in(key, 31), (REQS * MAXB, BLK, KVH, 2 * HD), jnp.float32)
    values = gaussian
    return jnp.clip(values, -4.0, 4.0).astype(jnp.bfloat16)


def draw_residual_in(key, part):
    row_scale = jnp.exp(jax.random.uniform(jax.random.fold_in(key, 41), (ROWS, 1), jnp.float32, -1.15, 1.15))
    column_scale = jnp.exp(jax.random.uniform(jax.random.fold_in(key, 42), (1, D), jnp.float32, -1.15, 1.15))
    values = 0.5 * jnp.clip(jax.random.normal(jax.random.fold_in(key, 44), (ROWS, D), jnp.float32), -3.0, 3.0)
    return jnp.clip(values * row_scale * column_scale, -16.0, 16.0).astype(jnp.bfloat16)


def draw_lengths(key, part):
    drawn = jax.random.randint(jax.random.fold_in(key, 51), (REQS,), NEW, MAXB * BLK + 1)
    longest = jax.random.randint(jax.random.fold_in(key, 52), (), 0, REQS)
    return drawn.at[longest].set(MAXB * BLK).astype(jnp.int32)


def draw_block_table(key, part):
    row_ids = jnp.arange(REQS, dtype=jnp.int32)

    def one_row(row_id):
        row_key = jax.random.fold_in(jax.random.fold_in(key, 61), row_id)
        raw = jax.random.randint(row_key, (MAXB,), 0, 1 << 20)
        distinct = raw * MAXB + jnp.arange(MAXB, dtype=jnp.int32)
        return jnp.argsort(distinct, stable=True).astype(jnp.int32)
    return jax.vmap(one_row)(row_ids).astype(jnp.int32)


def level_of(key, extent, cuts, smallest, largest):
    level, own = 1.0, jax.random.fold_in(key, 6)
    for position, parts in cuts:
        steps = jnp.exp(jax.random.uniform(jax.random.fold_in(own, position), (parts,), jnp.float32, smallest / len(cuts), largest / len(cuts)))
        level = level * jnp.repeat(steps, extent[position] // parts).reshape([-1 if axis == position else 1 for axis in range(len(extent))])
    return level


def deal_out(rng, own, number, rows, count, top, reach, skew):
    order = jax.random.permutation(rng, count)
    packed, usual = load_shares(count, rows * top, reach, skew, True), load_shares(count, rows * top, reach, skew, False)
    places = jnp.arange(count)

    def named(tallies, rotation):
        used = int((tallies > 0).sum())
        fixed = max(1, used // 4)
        passed = fixed + (places - fixed + rotation * (used - fixed)) % max(1, count - fixed)
        return jnp.zeros((count,), jnp.int32).at[order[jnp.where(places < fixed, places, passed)]].set(jnp.asarray(tallies, jnp.int32))

    tallies = jnp.where(number % 4 == 0, named(packed, number // 4), named(usual, number - number // 4 - 1))
    mixed = jax.random.permutation(jax.random.fold_in(own, 3), count)
    source_of, taker = mixed[0:count // 2 * 2:2], mixed[1:count // 2 * 2:2]
    slack = jnp.minimum(tallies[source_of] - 1, reach - tallies[taker]) // 2
    slack = jnp.where((source_of == order[0]) | (taker == order[0]) | (tallies[taker] == 0), 0, jnp.maximum(slack, 0))
    passed = jax.random.randint(jax.random.fold_in(own, 4), (count // 2,), 0, 1 << 20) % (slack + 1)
    tallies = tallies.at[source_of].add(-passed).at[taker].add(passed)
    items = jnp.searchsorted(jnp.cumsum(tallies), jnp.arange(rows * top), side="right").astype(jnp.int32)
    listing = items.reshape(top, rows).T
    listing = listing[jax.random.permutation(jax.random.fold_in(own, 1), rows)]
    rotation = jax.random.randint(jax.random.fold_in(own, 2), (rows, 1), 0, top)
    return jnp.take_along_axis(listing, (jnp.arange(top)[None, :] + rotation) % top, axis=1)


def load_shares(number_of, total, most, lean, full):
    portions = [(1 << 20) // math.isqrt(standing ** lean) + 1 for standing in range(1, number_of + 1)]
    largest = most if full else min(most, max(-(-total // number_of), total * portions[0] // sum(portions)))
    least = 1 if total - largest >= number_of - 1 else 0
    counts, rest = [largest] + [least] * (number_of - 1), total - largest - least * (number_of - 1)
    while rest > 0:
        candidates = [i for i in range(1, number_of) if counts[i] < largest] or [i for i in range(1, number_of) if counts[i] < most]
        mass, remaining = sum([portions[i] for i in candidates]), rest
        for i in candidates:
            addition = min(most - counts[i], max(1, remaining * portions[i] // mass), rest)
            counts[i] = counts[i] + addition
            rest = rest - addition
    return np.array(counts)


def centred(key, extent, deviation, bound, cuts=(), kind=jnp.bfloat16):
    loudness = level_of(key, extent, cuts, -0.22, 0.18) if cuts else 1.0
    values = jax.random.normal(key, extent, jnp.float32) * deviation * loudness
    return jnp.minimum(jnp.maximum(values, -bound), bound).astype(kind)


def setup_inputs(seed: int = 0, part: int = 0) -> dict:
    arg_keys = jax.random.split(jax.random.key(seed), 13)
    part_splits = jax.random.split(jax.random.fold_in(arg_keys[12], part), 13)
    queries = draw_queries(jax.random.fold_in(jax.random.fold_in(arg_keys[12], part), 71), part)
    cache_pool = draw_cache_pool(jax.random.fold_in(jax.random.fold_in(arg_keys[12], part), 71), part)
    lengths = draw_lengths(jax.random.fold_in(jax.random.fold_in(arg_keys[12], part), 71), part)
    block_table = draw_block_table(jax.random.fold_in(jax.random.fold_in(arg_keys[12], part), 71), part)
    out_proj = centred(arg_keys[4], (QH * HD, D), (QH * HD // 16) ** -0.5, 0.375, ((0, 8),))
    residual_in = draw_residual_in(jax.random.fold_in(jax.random.fold_in(arg_keys[12], part), 71), part)
    norm_gain = jnp.clip(1.0 + 0.18 * jax.random.normal(arg_keys[6], (D,), jnp.float32), 0.1, 1.9)
    expert_ids_keys = jax.random.split(jax.random.fold_in(part_splits[7], 1), ROWS // ROWS_DEV)
    expert_ids_turns = jax.random.permutation(jax.random.fold_in(part_splits[7], 3), ROWS // ROWS_DEV)
    expert_ids = jax.vmap(lambda own, number: deal_out(jax.random.fold_in(part_splits[7], 2), own, number, ROWS_DEV, EXPERTS, TOP, CAP, 2))(expert_ids_keys, expert_ids_turns).reshape((ROWS, TOP))
    route_weight = jnp.clip(0.2 + 0.8 * jax.random.uniform(part_splits[8], (ROWS, TOP), jnp.float32) ** level_of(part_splits[8], (ROWS, TOP), ((0, 16),), -0.2, 0.2), 0.2, 1.0)
    gate_weight = centred(arg_keys[9], (EXPERTS, D, HID), D ** -0.5, 0.109375, ((0, 8), (2, 2)))
    up_weight = centred(arg_keys[10], (EXPERTS, D, HID), D ** -0.5, 0.109375, ((0, 8), (2, 2)))
    down_weight = centred(arg_keys[11], (EXPERTS, HID, D), HID ** -0.5, 0.109375, ((0, 8), (1, 2)))
    return {"queries": queries, "cache_pool": cache_pool, "lengths": lengths, "block_table": block_table, "out_proj": out_proj, "residual_in": residual_in, "norm_gain": norm_gain, "expert_ids": expert_ids, "route_weight": route_weight, "gate_weight": gate_weight, "up_weight": up_weight, "down_weight": down_weight}


EPSILON = 1e-05
MASKED = -1e+30

def attend_request(query_rows, sequence, context):
    kv_of_head = jnp.arange(QH, dtype=jnp.int32) // (QH // KVH)
    key_heads = sequence[:, :, :HD][:, kv_of_head, :].astype(jnp.float32)
    value_heads = sequence[:, :, HD:][:, kv_of_head, :].astype(jnp.float32)
    scores = jnp.einsum('nhd,thd->hnt', query_rows.astype(jnp.float32), key_heads) * (1.0 / math.sqrt(HD))
    positions = context - NEW + jnp.arange(NEW, dtype=jnp.int32)
    key_positions = jnp.arange(MAXB * BLK, dtype=jnp.int32)
    visible = key_positions[None, None, :] <= positions[None, :, None]
    scores = jnp.where(visible, scores, MASKED)
    row_max = lax.optimization_barrier(jnp.max(scores, axis=-1, keepdims=True))
    exp_scores = jnp.exp(scores - row_max)
    row_sum = lax.optimization_barrier(jnp.sum(exp_scores, axis=-1, keepdims=True))
    probabilities = (exp_scores / row_sum).astype(jnp.bfloat16)
    attended = jnp.einsum('hnt,thd->nhd', probabilities.astype(jnp.float32), value_heads)
    return attended.astype(jnp.bfloat16).reshape(NEW, QH * HD)

def reference(queries, cache_pool, lengths, block_table, out_proj, residual_in, norm_gain, expert_ids, route_weight, gate_weight, up_weight, down_weight):

    def one_request(request):
        query_rows = lax.dynamic_slice_in_dim(queries, request * NEW, NEW, 0).reshape(NEW, QH, HD)
        block_ids = (request * MAXB + block_table[request]).astype(jnp.int32)
        sequence = cache_pool[block_ids].reshape(MAXB * BLK, KVH, 2 * HD)
        return attend_request(query_rows, sequence, lengths[request])
    attn = lax.map(one_request, jnp.arange(REQS, dtype=jnp.int32)).reshape(ROWS, QH * HD)
    group_width = QH * HD // QGROUPS

    def add_group(running, group):
        column_block = lax.dynamic_slice_in_dim(attn, group * group_width, group_width, 1)
        weight_block = lax.dynamic_slice_in_dim(out_proj, group * group_width, group_width, 0)
        partial_value = jnp.dot(column_block, weight_block, preferred_element_type=jnp.float32)
        partial_value = lax.optimization_barrier(partial_value.astype(jnp.bfloat16)).astype(jnp.float32)
        return (running + partial_value, None)
    projected, unused = lax.scan(add_group, jnp.zeros((ROWS, D), jnp.float32), jnp.arange(QGROUPS, dtype=jnp.int32))
    residual = (residual_in.astype(jnp.float32) + projected).astype(jnp.bfloat16)
    residual_wide = residual.astype(jnp.float32)
    mean_square = lax.optimization_barrier(jnp.mean(residual_wide * residual_wide, axis=-1, keepdims=True))
    normed = (residual_wide * lax.rsqrt(mean_square + EPSILON) * norm_gain).astype(jnp.bfloat16)
    per_expert = ROWS * TOP // EXPERTS
    sorted_order = jnp.argsort(expert_ids.reshape(-1), stable=True).astype(jnp.int32)
    rows_for = (sorted_order // TOP).astype(jnp.int32).reshape(EXPERTS, per_expert)
    weights_for = route_weight.reshape(-1)[sorted_order].reshape(EXPERTS, per_expert)
    shard_width = HID // HSHARDS

    def run_expert(expert):
        inputs = normed[rows_for[expert]]
        gate_out = jnp.dot(inputs, gate_weight[expert], preferred_element_type=jnp.float32)
        up_out = jnp.dot(inputs, up_weight[expert], preferred_element_type=jnp.float32)
        activated = (gate_out * jax.nn.sigmoid(1.702 * gate_out) * (up_out + 1.0)).astype(jnp.bfloat16)
        shards = activated.reshape(per_expert, HSHARDS, shard_width).astype(jnp.float32)
        down_shards = down_weight[expert].reshape(HSHARDS, shard_width, D).astype(jnp.float32)
        partial_value = jnp.einsum('pgs,gsd->gpd', shards, down_shards)
        partial_value = lax.optimization_barrier(partial_value.astype(jnp.bfloat16)).astype(jnp.float32)
        return lax.optimization_barrier(jnp.sum(partial_value, axis=0)).astype(jnp.bfloat16)
    expert_out = lax.map(run_expert, jnp.arange(EXPERTS, dtype=jnp.int32))
    weighted = weights_for[:, :, None] * expert_out.astype(jnp.float32)
    expert_mix = jnp.zeros((ROWS, D), jnp.float32).at[rows_for.reshape(-1)].add(weighted.reshape(-1, D))
    return (residual.astype(jnp.float32) + expert_mix).astype(jnp.bfloat16)
```

```python
import functools
import math

import jax
import jax.numpy as jnp
from jax import lax
from jax.experimental import pallas as pl
from jax.experimental.pallas import tpu as pltpu
from jax.sharding import PartitionSpec as P

QH = 64
KVH = 8
TOP = 4


EPSILON = 1e-05
MASKED = -1e30
CHUNK = 768


def run_expert(row_block, gate_weight, up_weight, down_weight):
    row_shape = row_block.shape
    flat_rows = row_block.reshape(-1, row_shape[-1])
    gate_out = jnp.dot(flat_rows, gate_weight[0], preferred_element_type=jnp.float32)
    up_out = jnp.dot(flat_rows, up_weight[0], preferred_element_type=jnp.float32)
    activated = (gate_out * jax.nn.sigmoid(1.702 * gate_out) * (up_out + 1.0)).astype(jnp.bfloat16)
    partial_value = jnp.dot(activated, down_weight[0], preferred_element_type=jnp.float32)
    return partial_value.astype(jnp.bfloat16).reshape(row_shape[:-1] + (partial_value.shape[-1],))


def masked_scores(query_heads, key_block, positions, score_scale):
    scores = (
        jnp.einsum("nhd,thd->hnt", query_heads, key_block, preferred_element_type=jnp.float32)
        * score_scale
    )
    key_positions = jnp.arange(key_block.shape[0], dtype=jnp.int32)
    visible = key_positions[None, None, :] <= positions[None, :, None]
    return jnp.where(visible, scores, MASKED)


def on_device(
    queries,
    cache_pool,
    lengths,
    block_table,
    out_proj,
    residual_in,
    norm_gain,
    expert_ids,
    route_weight,
    gate_weight,
    up_weight,
    down_weight,
):
    head_dim = cache_pool.shape[3] // 2
    block_len = cache_pool.shape[1]
    max_blocks = cache_pool.shape[0]
    new_rows = queries.shape[0]
    local_heads = queries.shape[1] // head_dim
    score_scale = 1.0 / math.sqrt(head_dim)
    context = lengths[0]
    sequence = cache_pool[block_table[0]]
    kv_choice = (
        lax.axis_index("sec") * local_heads + jnp.arange(local_heads, dtype=jnp.int32)
    ) // (QH // KVH)
    selected = jnp.take(sequence, kv_choice, axis=2)
    key_heads = selected[..., :head_dim]
    value_heads = selected[..., head_dim:]
    query_heads = queries.reshape(new_rows, local_heads, head_dim)
    positions = context - new_rows + jnp.arange(new_rows, dtype=jnp.int32)
    all_keys = key_heads.reshape(max_blocks * block_len, local_heads, head_dim)
    all_values = value_heads.reshape(max_blocks * block_len, local_heads, head_dim)
    scores = masked_scores(query_heads, all_keys, positions, score_scale)
    row_max = jnp.max(scores, axis=-1, keepdims=True)
    exp_scores = jnp.exp(scores - row_max)
    row_sum = jnp.sum(exp_scores, axis=-1, keepdims=True)
    probabilities = (exp_scores / row_sum).astype(jnp.bfloat16)
    attended = jnp.einsum(
        "hnt,thd->nhd", probabilities, all_values, preferred_element_type=jnp.float32
    )
    attn = attended.astype(jnp.bfloat16).reshape(new_rows, local_heads * head_dim)
    share_rows = new_rows // (lax.axis_size("head") * lax.axis_size("sec"))
    partial_value = jnp.dot(attn, out_proj, preferred_element_type=jnp.float32)
    projected = lax.psum_scatter(
        partial_value.astype(jnp.bfloat16).astype(jnp.float32).astype(jnp.bfloat16),
        ("head", "sec"),
        scatter_dimension=0,
        tiled=True,
    ).astype(jnp.float32)
    residual = (residual_in.astype(jnp.float32) + projected).astype(jnp.bfloat16)
    residual_wide = residual.astype(jnp.float32)
    mean_square = jnp.mean(residual_wide * residual_wide, axis=-1, keepdims=True)
    normed = (residual_wide * lax.rsqrt(mean_square + EPSILON) * norm_gain).astype(jnp.bfloat16)
    experts_all = lax.axis_size("head") * lax.axis_size("sec")
    capacity = share_rows * TOP // experts_all
    flat_ids = expert_ids.reshape(-1)
    onehot = (flat_ids[:, None] == jnp.arange(experts_all, dtype=jnp.int32)[None, :]).astype(
        jnp.int32
    )
    before = jnp.cumsum(onehot, axis=0) - onehot
    target = flat_ids * capacity + jnp.sum(before * onehot, axis=1)
    source_row = (
        jnp.zeros((experts_all * capacity,), jnp.int32)
        .at[target]
        .set(jnp.arange(share_rows * TOP, dtype=jnp.int32) // TOP)
    )
    buffer = normed[source_row].reshape(experts_all, capacity, normed.shape[1])
    copies = lax.all_gather(buffer[None], "req", axis=0, tiled=True)
    results = run_expert(
        lax.all_to_all(copies, ("head", "sec"), split_axis=1, concat_axis=1, tiled=True),
        gate_weight,
        up_weight,
        down_weight,
    )
    partial_back = lax.all_to_all(results, ("head", "sec"), split_axis=1, concat_axis=1, tiled=True)
    returned = (
        lax.psum_scatter(
            partial_back.astype(jnp.float32).astype(jnp.bfloat16),
            "req",
            scatter_dimension=0,
            tiled=True,
        )
        .astype(jnp.float32)[0]
        .astype(jnp.bfloat16)
    )
    gathered_out = returned.reshape(experts_all * capacity, -1)[target].reshape(share_rows, TOP, -1)
    expert_mix = jnp.sum(route_weight[:, :, None] * gathered_out.astype(jnp.float32), axis=1)
    return (residual.astype(jnp.float32) + expert_mix).astype(jnp.bfloat16)


def lane_chunks(width, size):
    return [(start, min(size, width - start)) for start in range(0, width, size)]


def layer_kernel(
    chunks,
    meta_col,
    experts,
    q_ref,
    kv_ref,
    len_ref,
    bt_ref,
    wo_ref,
    res_ref,
    gain_ref,
    ids_ref,
    rw_ref,
    wg_hbm,
    wu_hbm,
    wd_hbm,
    out_ref,
    wg,
    wu,
    wd,
    attn,
    psend,
    precv,
    pown,
    zsend,
    zrecv,
    resid,
    xbuf,
    xs,
    act,
    w_sem,
    core_send,
    core_recv,
    x_send,
    x_recv,
    z_send,
    z_recv,
    *chunk_refs,
):
    g, r = lax.axis_index("groups"), lax.axis_index("req")
    h, s = lax.axis_index("head"), lax.axis_index("sec")
    heads = attn.shape[0]
    share = attn.shape[2]
    depth = res_ref.shape[1]
    f32, bf16 = jnp.float32, jnp.bfloat16

    weight_copies = [
        pltpu.make_async_copy(src.at[0], dst, w_sem.at[i])
        for i, (src, dst) in enumerate(((wg_hbm, wg), (wu_hbm, wu), (wd_hbm, wd)))
    ]
    for copy in weight_copies:
        copy.start()

    core_dev = (g, r, h, 1 - s)
    x_dev = (g, 1 - r, h, s)
    z_devs = [(g, r, lax.rem(h + j, heads), s) for j in range(1, heads)]
    barrier = pltpu.get_barrier_semaphore()
    for device in [core_dev, x_dev] + z_devs:
        pl.semaphore_signal(
            barrier, inc=1, device_id=device, device_id_type=pl.DeviceIdType.MESH
        )

    def remote(src, dst, send_sem, recv_sem, device):
        return pltpu.make_async_remote_copy(
            src_ref=src,
            dst_ref=dst,
            send_sem=send_sem,
            recv_sem=recv_sem,
            device_id=device,
            device_id_type=pl.DeviceIdType.MESH,
        )

    tokens = kv_ref.shape[0]
    new_rows = q_ref.shape[0]
    blocks = bt_ref.shape[1]
    block_len = tokens // blocks
    lane_t = lax.broadcasted_iota(jnp.int32, (1, tokens), 1)
    stored = lane_t // block_len
    place = jnp.zeros((1, tokens), jnp.int32)
    for i in range(blocks):
        place = jnp.where(stored == bt_ref[0, i], i, place)
    key_pos = place * block_len + lane_t % block_len - (len_ref[0] - new_rows)
    row_pos = lax.broadcasted_iota(jnp.int32, (2 * new_rows, 1), 0) % new_rows
    visible = key_pos <= row_pos
    lane_q = lax.broadcasted_iota(jnp.int32, (new_rows, 128), 1)
    low = lane_q < 64
    for pair in range(q_ref.shape[1] // 128):
        both = q_ref[:, pair * 128 : (pair + 1) * 128].astype(f32) * 0.125
        even = jnp.where(low, both, 0.0)
        odd = jnp.where(low, pltpu.roll(both, 64, axis=1), 0.0)
        stacked = jnp.concatenate([even, odd], axis=0).astype(bf16)
        scores = lax.dot_general(
            stacked, kv_ref[...], (((1,), (1,)), ((), ())), preferred_element_type=f32
        )
        scores = jnp.where(visible, scores, MASKED)
        top = jnp.max(scores, axis=-1, keepdims=True)
        weights = jnp.exp(scores - top)
        total = jnp.sum(weights, axis=-1, keepdims=True)
        mixed = jnp.dot(weights.astype(bf16), kv_ref[...], preferred_element_type=f32) / total
        joined = jnp.where(low, pltpu.roll(mixed[:new_rows], 64, axis=1), mixed[new_rows:])
        attn[:, :, :, pair * 128 : (pair + 1) * 128] = joined.astype(bf16).reshape(
            heads, 2, share, 128
        )

    inner = attn.shape[3]
    psend[...] = jnp.dot(
        attn[:, 1 - s].reshape(heads * share, inner), wo_ref[...], preferred_element_type=f32
    ).astype(bf16)
    pl.semaphore_wait(barrier, 1 + heads)
    pair_copy = remote(psend, precv, core_send.at[0], core_recv.at[0], core_dev)
    pair_copy.start()
    pown[...] = jnp.dot(
        attn[:, s].reshape(heads * share, inner), wo_ref[...], preferred_element_type=f32
    ).reshape(heads, share, depth)
    pair_copy.wait_recv()
    pown[...] = pown[...] + precv[...].reshape(heads, share, depth).astype(f32)
    zsend[...] = pown[...].astype(bf16)
    order = sorted(range(1, heads), key=lambda j: -min(j, heads - j))
    z_copies = {}
    for j in order:
        z_copies[j] = remote(
            zsend.at[lax.rem(h + j, heads)],
            zrecv.at[j - 1],
            z_send.at[j - 1],
            z_recv.at[j - 1],
            z_devs[j - 1],
        )
        z_copies[j].start()
    sent = [pair_copy] + list(z_copies.values())

    lane_e = lax.broadcasted_iota(jnp.int32, (share, 128), 1)
    dense = jnp.zeros((share, 128), f32)
    for k in range(ids_ref.shape[1]):
        chosen = ids_ref[:, k : k + 1]
        dense = dense + jnp.where(
            (lane_e == chosen) | (lane_e == chosen + experts), rw_ref[:, k : k + 1], 0.0
        )
    coarse = dense.astype(bf16).astype(f32)
    meta = jnp.where(lane_e < experts, coarse, dense - coarse).astype(bf16)

    gathered = res_ref[...].astype(f32) + pown[h]
    for j in range(1, heads):
        z_copies[j].wait_recv()
        gathered = gathered + zrecv[j - 1].astype(f32)
    residual = gathered.astype(bf16)
    resid[...] = residual
    wide = residual.astype(f32)
    mean_square = jnp.mean(wide * wide, axis=-1, keepdims=True)
    normed = (wide * lax.rsqrt(mean_square + EPSILON) * gain_ref[...]).astype(bf16)
    xbuf[r, h, s, :, :depth] = normed
    xbuf[r, h, s, :, meta_col:] = meta

    def spread(rr, j, send_sem, recv_sem, device):
        block = xbuf.at[rr, lax.rem(h - j + heads, heads), s]
        return remote(block, block, send_sem, recv_sem, device)

    zg = {
        j: spread(r, 0, z_send.at[2 + j], z_recv.at[2 + j], z_devs[j - 1])
        for j in range(1, heads)
    }
    xg = {j: spread(r, j, x_send.at[j], x_recv.at[j], x_dev) for j in range(heads)}
    cg = {
        j: spread(r, j, core_send.at[1 + j], core_recv.at[1 + j], core_dev) for j in range(heads)
    }
    cx = {
        j: spread(
            1 - r, j, core_send.at[1 + heads + j], core_recv.at[1 + heads + j], core_dev
        )
        for j in range(heads)
    }
    for j in order:
        zg[j].start()
    xg[0].start()
    cg[0].start()
    near_first = order[::-1]
    for j in near_first:
        zg[j].wait_recv()
        xg[j].start()
        cg[j].start()
    for j in [0] + near_first:
        xg[j].wait_recv()
        cx[j].start()
    for j in range(heads):
        cg[j].wait_recv()
    for j in range(heads):
        cx[j].wait_recv()
    sent += list(zg.values()) + list(xg.values()) + list(cg.values()) + list(cx.values())

    half = 2 * heads * share
    xs[:half] = xbuf[:, :, 1 - s, :, :depth].reshape(half, depth)
    xs[half:] = xbuf[:, :, s, :, :depth].reshape(half, depth)
    expert = h * 2 + s
    lane_w = lax.broadcasted_iota(jnp.int32, (half, 128), 1)
    mine = (lane_w == expert) | (lane_w == expert + experts)

    def route_column(core):
        packed = xbuf[:, :, core, :, meta_col:].reshape(half, 128).astype(f32)
        return jnp.sum(jnp.where(mine, packed, 0.0), axis=-1, keepdims=True)

    other_weight = route_column(1 - s)
    own_weight = route_column(s)
    weight_copies[0].wait()
    weight_copies[1].wait()

    def hidden_tile(tile):
        gate_out = jnp.dot(xs[...], wg[:, tile], preferred_element_type=f32)
        up_out = jnp.dot(xs[...], wu[:, tile], preferred_element_type=f32)
        act[:, tile] = (gate_out * jax.nn.sigmoid(1.702 * gate_out) * (up_out + 1.0)).astype(bf16)

    hidden = wg.shape[1]
    full = hidden // 256

    @pl.loop(0, full)
    def _(i):
        hidden_tile(pl.ds(pl.multiple_of(i * 256, 256), 256))

    if hidden % 256:
        hidden_tile(pl.ds(full * 256, hidden % 256))
    weight_copies[2].wait()

    count = len(chunks)
    per = len(chunk_refs) // count
    base_core, base_x, base_z = 1 + 2 * heads, heads, 2 * (heads - 1)
    core_copies, x_copies, line_copies = {}, {}, {}

    def multiply(c):
        csend, crecv, cown, xsend, xrecv, zsend2, zrecv2 = chunk_refs[c * per : (c + 1) * per]
        start, width = chunks[c]
        product = jnp.dot(act[...], wd[:, start : start + width], preferred_element_type=f32)
        csend[...] = (product[:half] * other_weight).astype(bf16).reshape(2, heads, share, width)
        core_copies[c] = remote(
            csend, crecv, core_send.at[base_core + c], core_recv.at[base_core + c], core_dev
        )
        core_copies[c].start()
        cown[...] = (product[half:] * own_weight).reshape(2, heads, share, width)

    def over_core(c):
        csend, crecv, cown, xsend, xrecv, zsend2, zrecv2 = chunk_refs[c * per : (c + 1) * per]
        core_copies[c].wait_recv()
        xsend[...] = (cown[1 - r] + crecv[1 - r].astype(f32)).astype(bf16)
        x_copies[c] = remote(xsend, xrecv, x_send.at[base_x + c], x_recv.at[base_x + c], x_dev)
        x_copies[c].start()
        cown[r] = cown[r] + crecv[r].astype(f32)

    def over_req(c):
        csend, crecv, cown, xsend, xrecv, zsend2, zrecv2 = chunk_refs[c * per : (c + 1) * per]
        x_copies[c].wait_recv()
        cown[r] = cown[r] + xrecv[...].astype(f32)
        zsend2[...] = cown[r].astype(bf16)
        line_copies[c] = {}
        for j in order:
            sem = base_z + c * (heads - 1) + j - 1
            line_copies[c][j] = remote(
                zsend2.at[lax.rem(h + j, heads)],
                zrecv2.at[j - 1],
                z_send.at[sem],
                z_recv.at[sem],
                z_devs[j - 1],
            )
            line_copies[c][j].start()

    def over_line(c):
        csend, crecv, cown, xsend, xrecv, zsend2, zrecv2 = chunk_refs[c * per : (c + 1) * per]
        start, width = chunks[c]
        total = resid[:, start : start + width].astype(f32) + cown[r, h]
        for j in range(1, heads):
            line_copies[c][j].wait_recv()
            total = total + zrecv2[j - 1].astype(f32)
        out_ref[:, start : start + width] = total.astype(bf16)

    for step in range(count + 3):
        for lag, stage in enumerate((multiply, over_core, over_req, over_line)):
            if 0 <= step - lag < count:
                stage(step - lag)
    sent += list(core_copies.values()) + list(x_copies.values())
    for copies in line_copies.values():
        sent += list(copies.values())
    for copy in sent:
        copy.wait_send()


def fused_on_device(
    queries,
    cache_pool,
    lengths,
    block_table,
    out_proj,
    residual_in,
    norm_gain,
    expert_ids,
    route_weight,
    gate_weight,
    up_weight,
    down_weight,
):
    bf16, f32 = jnp.bfloat16, jnp.float32
    heads = lax.axis_size("head")
    share, depth = residual_in.shape
    inner = queries.shape[1]
    hidden = gate_weight.shape[2]
    experts = heads * 2
    tokens = cache_pool.shape[0] * cache_pool.shape[1]
    kv = lax.dynamic_index_in_dim(cache_pool, lax.axis_index("sec"), axis=2, keepdims=False)
    kv = kv.reshape(tokens, cache_pool.shape[3])
    meta_col = -(-depth // 128) * 128
    chunks = lane_chunks(depth, CHUNK)
    count = len(chunks)
    vmem = pltpu.VMEM
    scratch = [
        vmem((depth, hidden), bf16),
        vmem((depth, hidden), bf16),
        vmem((hidden, depth), bf16),
        vmem((heads, 2, share, inner), bf16),
        vmem((heads * share, depth), bf16),
        vmem((heads * share, depth), bf16),
        vmem((heads, share, depth), f32),
        vmem((heads, share, depth), bf16),
        vmem((heads - 1, share, depth), bf16),
        vmem((share, depth), bf16),
        vmem((2, heads, 2, share, meta_col + 128), bf16),
        vmem((4 * heads * share, depth), bf16),
        vmem((4 * heads * share, hidden), bf16),
        pltpu.SemaphoreType.DMA((3,)),
        pltpu.SemaphoreType.DMA((1 + 2 * heads + count,)),
        pltpu.SemaphoreType.DMA((1 + 2 * heads + count,)),
        pltpu.SemaphoreType.DMA((heads + count,)),
        pltpu.SemaphoreType.DMA((heads + count,)),
        pltpu.SemaphoreType.DMA(((heads - 1) * (2 + count),)),
        pltpu.SemaphoreType.DMA(((heads - 1) * (2 + count),)),
    ]
    for start, width in chunks:
        scratch += [
            vmem((2, heads, share, width), bf16),
            vmem((2, heads, share, width), bf16),
            vmem((2, heads, share, width), f32),
            vmem((heads, share, width), bf16),
            vmem((heads, share, width), bf16),
            vmem((heads, share, width), bf16),
            vmem((heads - 1, share, width), bf16),
        ]
    in_vmem = pl.BlockSpec(memory_space=pltpu.VMEM)
    in_smem = pl.BlockSpec(memory_space=pltpu.SMEM)
    in_place = pl.BlockSpec(memory_space=pl.ANY)
    return pl.pallas_call(
        functools.partial(layer_kernel, chunks, meta_col, experts),
        out_shape=jax.ShapeDtypeStruct((share, depth), bf16),
        in_specs=[in_vmem, in_vmem, in_smem, in_smem] + [in_vmem] * 5 + [in_place] * 3,
        out_specs=in_vmem,
        scratch_shapes=scratch,
        compiler_params=pltpu.CompilerParams(
            collective_id=0, has_side_effects=True, vmem_limit_bytes=58 << 20
        ),
    )(
        queries,
        kv,
        lengths,
        block_table,
        out_proj,
        residual_in,
        norm_gain[None, :],
        expert_ids,
        route_weight,
        gate_weight,
        up_weight,
        down_weight,
    )


def solution(mesh):
    sizes = dict(mesh.shape)
    fused = sizes["req"] == 2 and sizes["sec"] == 2 and sizes["head"] == 4
    return jax.shard_map(
        fused_on_device if fused else on_device,
        mesh=mesh,
        in_specs=(
            P(("groups", "req"), ("head", "sec")),
            P(("groups", "req"), None, "head", None),
            P(("groups", "req")),
            P(("groups", "req"), None),
            P(("head", "sec"), None),
            P(("groups", "req", "head", "sec"), None),
            P(),
            P(("groups", "req", "head", "sec"), None),
            P(("groups", "req", "head", "sec"), None),
            P(("head", "sec"), None, "req"),
            P(("head", "sec"), None, "req"),
            P(("head", "sec"), "req", None),
        ),
        out_specs=P(("groups", "req", "head", "sec"), None),
        check_vma=False,
    )
```

```python
import functools
import math

import jax
import jax.numpy as jnp
from jax import lax
from jax.experimental import pallas as pl
from jax.experimental.pallas import tpu as pltpu
from jax.sharding import PartitionSpec as P

QH = 64
KVH = 8
TOP = 4


EPSILON = 1e-05
MASKED = -1e30
CHUNK = 768


def run_expert(row_block, gate_weight, up_weight, down_weight):
    row_shape = row_block.shape
    flat_rows = row_block.reshape(-1, row_shape[-1])
    gate_out = jnp.dot(flat_rows, gate_weight[0], preferred_element_type=jnp.float32)
    up_out = jnp.dot(flat_rows, up_weight[0], preferred_element_type=jnp.float32)
    activated = (gate_out * jax.nn.sigmoid(1.702 * gate_out) * (up_out + 1.0)).astype(jnp.bfloat16)
    partial_value = jnp.dot(activated, down_weight[0], preferred_element_type=jnp.float32)
    return partial_value.astype(jnp.bfloat16).reshape(row_shape[:-1] + (partial_value.shape[-1],))


def masked_scores(query_heads, key_block, positions, score_scale):
    scores = (
        jnp.einsum("nhd,thd->hnt", query_heads, key_block, preferred_element_type=jnp.float32)
        * score_scale
    )
    key_positions = jnp.arange(key_block.shape[0], dtype=jnp.int32)
    visible = key_positions[None, None, :] <= positions[None, :, None]
    return jnp.where(visible, scores, MASKED)


def on_device(
    queries,
    cache_pool,
    lengths,
    block_table,
    out_proj,
    residual_in,
    norm_gain,
    expert_ids,
    route_weight,
    gate_weight,
    up_weight,
    down_weight,
):
    head_dim = cache_pool.shape[3] // 2
    block_len = cache_pool.shape[1]
    max_blocks = cache_pool.shape[0]
    new_rows = queries.shape[0]
    local_heads = queries.shape[1] // head_dim
    score_scale = 1.0 / math.sqrt(head_dim)
    context = lengths[0]
    sequence = cache_pool[block_table[0]]
    kv_choice = (
        lax.axis_index("sec") * local_heads + jnp.arange(local_heads, dtype=jnp.int32)
    ) // (QH // KVH)
    selected = jnp.take(sequence, kv_choice, axis=2)
    key_heads = selected[..., :head_dim]
    value_heads = selected[..., head_dim:]
    query_heads = queries.reshape(new_rows, local_heads, head_dim)
    positions = context - new_rows + jnp.arange(new_rows, dtype=jnp.int32)
    all_keys = key_heads.reshape(max_blocks * block_len, local_heads, head_dim)
    all_values = value_heads.reshape(max_blocks * block_len, local_heads, head_dim)
    scores = masked_scores(query_heads, all_keys, positions, score_scale)
    row_max = jnp.max(scores, axis=-1, keepdims=True)
    exp_scores = jnp.exp(scores - row_max)
    row_sum = jnp.sum(exp_scores, axis=-1, keepdims=True)
    probabilities = (exp_scores / row_sum).astype(jnp.bfloat16)
    attended = jnp.einsum(
        "hnt,thd->nhd", probabilities, all_values, preferred_element_type=jnp.float32
    )
    attn = attended.astype(jnp.bfloat16).reshape(new_rows, local_heads * head_dim)
    share_rows = new_rows // (lax.axis_size("head") * lax.axis_size("sec"))
    partial_value = jnp.dot(attn, out_proj, preferred_element_type=jnp.float32)
    projected = lax.psum_scatter(
        partial_value.astype(jnp.bfloat16).astype(jnp.float32).astype(jnp.bfloat16),
        ("head", "sec"),
        scatter_dimension=0,
        tiled=True,
    ).astype(jnp.float32)
    residual = (residual_in.astype(jnp.float32) + projected).astype(jnp.bfloat16)
    residual_wide = residual.astype(jnp.float32)
    mean_square = jnp.mean(residual_wide * residual_wide, axis=-1, keepdims=True)
    normed = (residual_wide * lax.rsqrt(mean_square + EPSILON) * norm_gain).astype(jnp.bfloat16)
    experts_all = lax.axis_size("head") * lax.axis_size("sec")
    capacity = share_rows * TOP // experts_all
    flat_ids = expert_ids.reshape(-1)
    onehot = (flat_ids[:, None] == jnp.arange(experts_all, dtype=jnp.int32)[None, :]).astype(
        jnp.int32
    )
    before = jnp.cumsum(onehot, axis=0) - onehot
    target = flat_ids * capacity + jnp.sum(before * onehot, axis=1)
    source_row = (
        jnp.zeros((experts_all * capacity,), jnp.int32)
        .at[target]
        .set(jnp.arange(share_rows * TOP, dtype=jnp.int32) // TOP)
    )
    buffer = normed[source_row].reshape(experts_all, capacity, normed.shape[1])
    copies = lax.all_gather(buffer[None], "req", axis=0, tiled=True)
    results = run_expert(
        lax.all_to_all(copies, ("head", "sec"), split_axis=1, concat_axis=1, tiled=True),
        gate_weight,
        up_weight,
        down_weight,
    )
    partial_back = lax.all_to_all(results, ("head", "sec"), split_axis=1, concat_axis=1, tiled=True)
    returned = (
        lax.psum_scatter(
            partial_back.astype(jnp.float32).astype(jnp.bfloat16),
            "req",
            scatter_dimension=0,
            tiled=True,
        )
        .astype(jnp.float32)[0]
        .astype(jnp.bfloat16)
    )
    gathered_out = returned.reshape(experts_all * capacity, -1)[target].reshape(share_rows, TOP, -1)
    expert_mix = jnp.sum(route_weight[:, :, None] * gathered_out.astype(jnp.float32), axis=1)
    return (residual.astype(jnp.float32) + expert_mix).astype(jnp.bfloat16)


def lane_chunks(width, size):
    return [(start, min(size, width - start)) for start in range(0, width, size)]


def dot_rows(rows, weight_rows):
    return lax.dot_general(
        rows, weight_rows, (((1,), (1,)), ((), ())), preferred_element_type=jnp.float32
    )


def layer_kernel(
    chunks,
    meta_col,
    experts,
    q_ref,
    kv_ref,
    len_ref,
    bt_ref,
    wo_ref,
    res_ref,
    gain_ref,
    ids_ref,
    rw_ref,
    wg_hbm,
    wu_hbm,
    wd_hbm,
    out_ref,
    wg,
    wu,
    wd,
    attn,
    psend,
    precv,
    pown,
    zsend,
    zrecv,
    resid,
    xbuf,
    xs,
    act,
    w_sem,
    core_send,
    core_recv,
    x_send,
    x_recv,
    z_send,
    z_recv,
    *chunk_refs,
):
    g, r = lax.axis_index("groups"), lax.axis_index("req")
    h, s = lax.axis_index("head"), lax.axis_index("sec")
    heads = attn.shape[0]
    share = attn.shape[2]
    depth = res_ref.shape[1]
    f32, bf16 = jnp.float32, jnp.bfloat16

    weight_copies = [
        pltpu.make_async_copy(src.at[0], dst, w_sem.at[i])
        for i, (src, dst) in enumerate(((wg_hbm, wg), (wu_hbm, wu), (wd_hbm, wd)))
    ]
    for copy in weight_copies:
        copy.start()

    core_dev = (g, r, h, 1 - s)
    x_dev = (g, 1 - r, h, s)
    z_devs = [(g, r, lax.rem(h + j, heads), s) for j in range(1, heads)]
    barrier = pltpu.get_barrier_semaphore()
    for device in [core_dev, x_dev] + z_devs:
        pl.semaphore_signal(
            barrier, inc=1, device_id=device, device_id_type=pl.DeviceIdType.MESH
        )

    def remote(src, dst, send_sem, recv_sem, device):
        return pltpu.make_async_remote_copy(
            src_ref=src,
            dst_ref=dst,
            send_sem=send_sem,
            recv_sem=recv_sem,
            device_id=device,
            device_id_type=pl.DeviceIdType.MESH,
        )

    tokens = kv_ref.shape[0]
    new_rows = q_ref.shape[0]
    blocks = bt_ref.shape[1]
    block_len = tokens // blocks
    lane_t = lax.broadcasted_iota(jnp.int32, (1, tokens), 1)
    stored = lane_t // block_len
    place = jnp.zeros((1, tokens), jnp.int32)
    for i in range(blocks):
        place = jnp.where(stored == bt_ref[0, i], i, place)
    key_pos = place * block_len + lane_t % block_len - (len_ref[0] - new_rows)
    row_pos = lax.broadcasted_iota(jnp.int32, (2 * new_rows, 1), 0) % new_rows
    visible = key_pos <= row_pos
    lane_q = lax.broadcasted_iota(jnp.int32, (new_rows, 128), 1)
    low = lane_q < 64
    for pair in range(q_ref.shape[1] // 128):
        both = q_ref[:, pair * 128 : (pair + 1) * 128].astype(f32) * 0.125
        even = jnp.where(low, both, 0.0)
        odd = jnp.where(low, pltpu.roll(both, 64, axis=1), 0.0)
        stacked = jnp.concatenate([even, odd], axis=0).astype(bf16)
        scores = dot_rows(stacked, kv_ref[...])
        scores = jnp.where(visible, scores, MASKED)
        top = jnp.max(scores, axis=-1, keepdims=True)
        weights = jnp.exp(scores - top)
        total = jnp.sum(weights, axis=-1, keepdims=True)
        mixed = jnp.dot(weights.astype(bf16), kv_ref[...], preferred_element_type=f32) / total
        joined = jnp.where(low, pltpu.roll(mixed[:new_rows], 64, axis=1), mixed[new_rows:])
        attn[:, :, :, pair * 128 : (pair + 1) * 128] = joined.astype(bf16).reshape(
            heads, 2, share, 128
        )

    inner = attn.shape[3]
    psend[...] = dot_rows(attn[:, 1 - s].reshape(heads * share, inner), wo_ref[...]).astype(bf16)
    pl.semaphore_wait(barrier, 1 + heads)
    pair_copy = remote(psend, precv, core_send.at[0], core_recv.at[0], core_dev)
    pair_copy.start()
    pown[...] = dot_rows(attn[:, s].reshape(heads * share, inner), wo_ref[...]).reshape(
        heads, share, depth
    )
    pair_copy.wait_recv()
    pown[...] = pown[...] + precv[...].reshape(heads, share, depth).astype(f32)
    zsend[...] = pown[...].astype(bf16)
    order = sorted(range(1, heads), key=lambda j: -min(j, heads - j))
    z_copies = {}
    for j in order:
        z_copies[j] = remote(
            zsend.at[lax.rem(h + j, heads)],
            zrecv.at[j - 1],
            z_send.at[j - 1],
            z_recv.at[j - 1],
            z_devs[j - 1],
        )
        z_copies[j].start()
    sent = [pair_copy] + list(z_copies.values())

    lane_e = lax.broadcasted_iota(jnp.int32, (share, 128), 1)
    line_e = lax.broadcasted_iota(jnp.int32, (128, share), 0)
    by_expert = jnp.zeros((128, share), f32)
    for k in range(ids_ref.shape[0]):
        chosen = ids_ref[k : k + 1, :]
        by_expert = by_expert + jnp.where(
            (line_e == chosen) | (line_e == chosen + experts), rw_ref[k : k + 1, :], 0.0
        )
    dense = by_expert.T
    coarse = dense.astype(bf16).astype(f32)
    meta = jnp.where(lane_e < experts, coarse, dense - coarse).astype(bf16)

    gathered = res_ref[...].astype(f32) + pown[h]
    for j in range(1, heads):
        z_copies[j].wait_recv()
        gathered = gathered + zrecv[j - 1].astype(f32)
    residual = gathered.astype(bf16)
    resid[...] = residual
    wide = residual.astype(f32)
    mean_square = jnp.mean(wide * wide, axis=-1, keepdims=True)
    normed = (wide * lax.rsqrt(mean_square + EPSILON) * gain_ref[...][None, :]).astype(bf16)
    xbuf[r, h, s, :, :depth] = normed
    xbuf[r, h, s, :, meta_col:] = meta

    def spread(rr, j, send_sem, recv_sem, device):
        block = xbuf.at[rr, lax.rem(h - j + heads, heads), s]
        return remote(block, block, send_sem, recv_sem, device)

    zg = {
        j: spread(r, 0, z_send.at[2 + j], z_recv.at[2 + j], z_devs[j - 1])
        for j in range(1, heads)
    }
    xg = {j: spread(r, j, x_send.at[j], x_recv.at[j], x_dev) for j in range(heads)}
    cg = {
        j: spread(r, j, core_send.at[1 + j], core_recv.at[1 + j], core_dev) for j in range(heads)
    }
    cx = {
        j: spread(
            1 - r, j, core_send.at[1 + heads + j], core_recv.at[1 + heads + j], core_dev
        )
        for j in range(heads)
    }
    for j in order:
        zg[j].start()
    xg[0].start()
    cg[0].start()
    near_first = order[::-1]
    for j in near_first:
        zg[j].wait_recv()
        xg[j].start()
        cg[j].start()
    for j in [0] + near_first:
        xg[j].wait_recv()
        cx[j].start()
    for j in range(heads):
        cg[j].wait_recv()
    for j in range(heads):
        cx[j].wait_recv()
    sent += list(zg.values()) + list(xg.values()) + list(cg.values()) + list(cx.values())

    half = 2 * heads * share
    xs[:half] = xbuf[:, :, 1 - s, :, :depth].reshape(half, depth)
    xs[half:] = xbuf[:, :, s, :, :depth].reshape(half, depth)
    expert = h * 2 + s
    lane_w = lax.broadcasted_iota(jnp.int32, (half, 128), 1)
    mine = (lane_w == expert) | (lane_w == expert + experts)

    def route_column(core):
        packed = xbuf[:, :, core, :, meta_col:].reshape(half, 128).astype(f32)
        return jnp.sum(jnp.where(mine, packed, 0.0), axis=-1, keepdims=True)

    other_weight = route_column(1 - s)
    own_weight = route_column(s)
    weight_copies[0].wait()
    weight_copies[1].wait()

    def hidden_tile(tile):
        gate_out = dot_rows(xs[...], wg[tile, :])
        up_out = dot_rows(xs[...], wu[tile, :])
        act[:, tile] = (gate_out * jax.nn.sigmoid(1.702 * gate_out) * (up_out + 1.0)).astype(bf16)

    hidden = wg.shape[0]
    full = hidden // 256

    @pl.loop(0, full)
    def _(i):
        hidden_tile(pl.ds(pl.multiple_of(i * 256, 256), 256))

    if hidden % 256:
        hidden_tile(pl.ds(full * 256, hidden % 256))
    weight_copies[2].wait()

    count = len(chunks)
    per = len(chunk_refs) // count
    base_core, base_x, base_z = 1 + 2 * heads, heads, 2 * (heads - 1)
    core_copies, x_copies, line_copies = {}, {}, {}

    def multiply(c):
        csend, crecv, cown, xsend, xrecv, zsend2, zrecv2 = chunk_refs[c * per : (c + 1) * per]
        start, width = chunks[c]
        product = jnp.dot(act[...], wd[:, start : start + width], preferred_element_type=f32)
        csend[...] = (product[:half] * other_weight).astype(bf16).reshape(2, heads, share, width)
        core_copies[c] = remote(
            csend, crecv, core_send.at[base_core + c], core_recv.at[base_core + c], core_dev
        )
        core_copies[c].start()
        cown[...] = (product[half:] * own_weight).reshape(2, heads, share, width)

    def over_core(c):
        csend, crecv, cown, xsend, xrecv, zsend2, zrecv2 = chunk_refs[c * per : (c + 1) * per]
        core_copies[c].wait_recv()
        xsend[...] = (cown[1 - r] + crecv[1 - r].astype(f32)).astype(bf16)
        x_copies[c] = remote(xsend, xrecv, x_send.at[base_x + c], x_recv.at[base_x + c], x_dev)
        x_copies[c].start()
        cown[r] = cown[r] + crecv[r].astype(f32)

    def over_req(c):
        csend, crecv, cown, xsend, xrecv, zsend2, zrecv2 = chunk_refs[c * per : (c + 1) * per]
        x_copies[c].wait_recv()
        cown[r] = cown[r] + xrecv[...].astype(f32)
        zsend2[...] = cown[r].astype(bf16)
        line_copies[c] = {}
        for j in order:
            sem = base_z + c * (heads - 1) + j - 1
            line_copies[c][j] = remote(
                zsend2.at[lax.rem(h + j, heads)],
                zrecv2.at[j - 1],
                z_send.at[sem],
                z_recv.at[sem],
                z_devs[j - 1],
            )
            line_copies[c][j].start()

    def over_line(c):
        csend, crecv, cown, xsend, xrecv, zsend2, zrecv2 = chunk_refs[c * per : (c + 1) * per]
        start, width = chunks[c]
        total = resid[:, start : start + width].astype(f32) + cown[r, h]
        for j in range(1, heads):
            line_copies[c][j].wait_recv()
            total = total + zrecv2[j - 1].astype(f32)
        out_ref[:, start : start + width] = total.astype(bf16)

    for step in range(count + 3):
        for lag, stage in enumerate((multiply, over_core, over_req, over_line)):
            if 0 <= step - lag < count:
                stage(step - lag)
    sent += list(core_copies.values()) + list(x_copies.values())
    for copies in line_copies.values():
        sent += list(copies.values())
    for copy in sent:
        copy.wait_send()


def fused_on_device(
    queries,
    cache_pool,
    lengths,
    block_table,
    out_proj,
    residual_in,
    norm_gain,
    expert_ids,
    route_weight,
    gate_weight,
    up_weight,
    down_weight,
):
    bf16, f32 = jnp.bfloat16, jnp.float32
    heads = lax.axis_size("head")
    share, depth = residual_in.shape
    inner = queries.shape[1]
    hidden = gate_weight.shape[2]
    experts = heads * 2
    tokens = cache_pool.shape[0] * cache_pool.shape[1]
    kv = lax.dynamic_index_in_dim(cache_pool, lax.axis_index("sec"), axis=2, keepdims=False)
    kv = kv.reshape(tokens, cache_pool.shape[3])
    meta_col = -(-depth // 128) * 128
    chunks = lane_chunks(depth, CHUNK)
    count = len(chunks)
    vmem = pltpu.VMEM
    scratch = [
        vmem((hidden, depth), bf16),
        vmem((hidden, depth), bf16),
        vmem((hidden, depth), bf16),
        vmem((heads, 2, share, inner), bf16),
        vmem((heads * share, depth), bf16),
        vmem((heads * share, depth), bf16),
        vmem((heads, share, depth), f32),
        vmem((heads, share, depth), bf16),
        vmem((heads - 1, share, depth), bf16),
        vmem((share, depth), bf16),
        vmem((2, heads, 2, share, meta_col + 128), bf16),
        vmem((4 * heads * share, depth), bf16),
        vmem((4 * heads * share, hidden), bf16),
        pltpu.SemaphoreType.DMA((3,)),
        pltpu.SemaphoreType.DMA((1 + 2 * heads + count,)),
        pltpu.SemaphoreType.DMA((1 + 2 * heads + count,)),
        pltpu.SemaphoreType.DMA((heads + count,)),
        pltpu.SemaphoreType.DMA((heads + count,)),
        pltpu.SemaphoreType.DMA(((heads - 1) * (2 + count),)),
        pltpu.SemaphoreType.DMA(((heads - 1) * (2 + count),)),
    ]
    for start, width in chunks:
        scratch += [
            vmem((2, heads, share, width), bf16),
            vmem((2, heads, share, width), bf16),
            vmem((2, heads, share, width), f32),
            vmem((heads, share, width), bf16),
            vmem((heads, share, width), bf16),
            vmem((heads, share, width), bf16),
            vmem((heads - 1, share, width), bf16),
        ]
    in_vmem = pl.BlockSpec(memory_space=pltpu.VMEM)
    in_smem = pl.BlockSpec(memory_space=pltpu.SMEM)
    in_place = pl.BlockSpec(memory_space=pl.ANY)
    return pl.pallas_call(
        functools.partial(layer_kernel, chunks, meta_col, experts),
        out_shape=jax.ShapeDtypeStruct((share, depth), bf16),
        in_specs=[in_vmem, in_vmem, in_smem, in_smem] + [in_vmem] * 5 + [in_place] * 3,
        out_specs=in_vmem,
        scratch_shapes=scratch,
        compiler_params=pltpu.CompilerParams(
            collective_id=0, has_side_effects=True, vmem_limit_bytes=58 << 20
        ),
    )(
        queries,
        kv,
        lengths,
        block_table,
        out_proj.T,
        residual_in,
        norm_gain,
        expert_ids.T,
        route_weight.T,
        jnp.swapaxes(gate_weight, 1, 2),
        jnp.swapaxes(up_weight, 1, 2),
        down_weight,
    )


def solution(mesh):
    sizes = dict(mesh.shape)
    fused = sizes["req"] == 2 and sizes["sec"] == 2 and sizes["head"] == 4
    return jax.shard_map(
        fused_on_device if fused else on_device,
        mesh=mesh,
        in_specs=(
            P(("groups", "req"), ("head", "sec")),
            P(("groups", "req"), None, "head", None),
            P(("groups", "req")),
            P(("groups", "req"), None),
            P(("head", "sec"), None),
            P(("groups", "req", "head", "sec"), None),
            P(),
            P(("groups", "req", "head", "sec"), None),
            P(("groups", "req", "head", "sec"), None),
            P(("head", "sec"), None, "req"),
            P(("head", "sec"), None, "req"),
            P(("head", "sec"), "req", None),
        ),
        out_specs=P(("groups", "req", "head", "sec"), None),
        check_vma=False,
    )
```

```python
import functools
import math

import jax
import jax.numpy as jnp
from jax import lax
from jax.experimental import pallas as pl
from jax.experimental.pallas import tpu as pltpu
from jax.sharding import PartitionSpec as P

QH = 64
KVH = 8
TOP = 4


EPSILON = 1e-05
MASKED = -1e30
CHUNK = 768


def run_expert(row_block, gate_weight, up_weight, down_weight):
    row_shape = row_block.shape
    flat_rows = row_block.reshape(-1, row_shape[-1])
    gate_out = jnp.dot(flat_rows, gate_weight[0], preferred_element_type=jnp.float32)
    up_out = jnp.dot(flat_rows, up_weight[0], preferred_element_type=jnp.float32)
    activated = (gate_out * jax.nn.sigmoid(1.702 * gate_out) * (up_out + 1.0)).astype(jnp.bfloat16)
    partial_value = jnp.dot(activated, down_weight[0], preferred_element_type=jnp.float32)
    return partial_value.astype(jnp.bfloat16).reshape(row_shape[:-1] + (partial_value.shape[-1],))


def masked_scores(query_heads, key_block, positions, score_scale):
    scores = (
        jnp.einsum("nhd,thd->hnt", query_heads, key_block, preferred_element_type=jnp.float32)
        * score_scale
    )
    key_positions = jnp.arange(key_block.shape[0], dtype=jnp.int32)
    visible = key_positions[None, None, :] <= positions[None, :, None]
    return jnp.where(visible, scores, MASKED)


def on_device(
    queries,
    cache_pool,
    lengths,
    block_table,
    out_proj,
    residual_in,
    norm_gain,
    expert_ids,
    route_weight,
    gate_weight,
    up_weight,
    down_weight,
):
    head_dim = cache_pool.shape[3] // 2
    block_len = cache_pool.shape[1]
    max_blocks = cache_pool.shape[0]
    new_rows = queries.shape[0]
    local_heads = queries.shape[1] // head_dim
    score_scale = 1.0 / math.sqrt(head_dim)
    context = lengths[0]
    sequence = cache_pool[block_table[0]]
    kv_choice = (
        lax.axis_index("sec") * local_heads + jnp.arange(local_heads, dtype=jnp.int32)
    ) // (QH // KVH)
    selected = jnp.take(sequence, kv_choice, axis=2)
    key_heads = selected[..., :head_dim]
    value_heads = selected[..., head_dim:]
    query_heads = queries.reshape(new_rows, local_heads, head_dim)
    positions = context - new_rows + jnp.arange(new_rows, dtype=jnp.int32)
    all_keys = key_heads.reshape(max_blocks * block_len, local_heads, head_dim)
    all_values = value_heads.reshape(max_blocks * block_len, local_heads, head_dim)
    scores = masked_scores(query_heads, all_keys, positions, score_scale)
    row_max = jnp.max(scores, axis=-1, keepdims=True)
    exp_scores = jnp.exp(scores - row_max)
    row_sum = jnp.sum(exp_scores, axis=-1, keepdims=True)
    probabilities = (exp_scores / row_sum).astype(jnp.bfloat16)
    attended = jnp.einsum(
        "hnt,thd->nhd", probabilities, all_values, preferred_element_type=jnp.float32
    )
    attn = attended.astype(jnp.bfloat16).reshape(new_rows, local_heads * head_dim)
    share_rows = new_rows // (lax.axis_size("head") * lax.axis_size("sec"))
    partial_value = jnp.dot(attn, out_proj, preferred_element_type=jnp.float32)
    projected = lax.psum_scatter(
        partial_value.astype(jnp.bfloat16).astype(jnp.float32).astype(jnp.bfloat16),
        ("head", "sec"),
        scatter_dimension=0,
        tiled=True,
    ).astype(jnp.float32)
    residual = (residual_in.astype(jnp.float32) + projected).astype(jnp.bfloat16)
    residual_wide = residual.astype(jnp.float32)
    mean_square = jnp.mean(residual_wide * residual_wide, axis=-1, keepdims=True)
    normed = (residual_wide * lax.rsqrt(mean_square + EPSILON) * norm_gain).astype(jnp.bfloat16)
    experts_all = lax.axis_size("head") * lax.axis_size("sec")
    capacity = share_rows * TOP // experts_all
    flat_ids = expert_ids.reshape(-1)
    onehot = (flat_ids[:, None] == jnp.arange(experts_all, dtype=jnp.int32)[None, :]).astype(
        jnp.int32
    )
    before = jnp.cumsum(onehot, axis=0) - onehot
    target = flat_ids * capacity + jnp.sum(before * onehot, axis=1)
    source_row = (
        jnp.zeros((experts_all * capacity,), jnp.int32)
        .at[target]
        .set(jnp.arange(share_rows * TOP, dtype=jnp.int32) // TOP)
    )
    buffer = normed[source_row].reshape(experts_all, capacity, normed.shape[1])
    copies = lax.all_gather(buffer[None], "req", axis=0, tiled=True)
    results = run_expert(
        lax.all_to_all(copies, ("head", "sec"), split_axis=1, concat_axis=1, tiled=True),
        gate_weight,
        up_weight,
        down_weight,
    )
    partial_back = lax.all_to_all(results, ("head", "sec"), split_axis=1, concat_axis=1, tiled=True)
    returned = (
        lax.psum_scatter(
            partial_back.astype(jnp.float32).astype(jnp.bfloat16),
            "req",
            scatter_dimension=0,
            tiled=True,
        )
        .astype(jnp.float32)[0]
        .astype(jnp.bfloat16)
    )
    gathered_out = returned.reshape(experts_all * capacity, -1)[target].reshape(share_rows, TOP, -1)
    expert_mix = jnp.sum(route_weight[:, :, None] * gathered_out.astype(jnp.float32), axis=1)
    return (residual.astype(jnp.float32) + expert_mix).astype(jnp.bfloat16)


def lane_chunks(width, size):
    return [(start, min(size, width - start)) for start in range(0, width, size)]


def dot_rows(rows, weight_rows):
    return lax.dot_general(
        rows, weight_rows, (((1,), (1,)), ((), ())), preferred_element_type=jnp.float32
    )


def layer_kernel(
    chunks,
    q_ref,
    kv_ref,
    len_ref,
    bt_ref,
    wo_ref,
    res_ref,
    gain_ref,
    ids_ref,
    rw_ref,
    wg_hbm,
    wu_hbm,
    wd_hbm,
    out_ref,
    wg,
    wu,
    wd,
    attn,
    psend,
    precv,
    pown,
    zsend,
    zrecv,
    resid,
    disp,
    xin,
    act,
    w_sem,
    core_send,
    core_recv,
    x_send,
    x_recv,
    z_send,
    z_recv,
    *chunk_refs,
):
    g, r = lax.axis_index("groups"), lax.axis_index("req")
    h, s = lax.axis_index("head"), lax.axis_index("sec")
    heads = attn.shape[0]
    share = attn.shape[2]
    depth = res_ref.shape[1]
    cap = disp.shape[2]
    f32, bf16 = jnp.float32, jnp.bfloat16

    weight_copies = [
        pltpu.make_async_copy(src.at[0], dst, w_sem.at[i])
        for i, (src, dst) in enumerate(((wg_hbm, wg), (wu_hbm, wu), (wd_hbm, wd)))
    ]
    for copy in weight_copies:
        copy.start()

    core_dev = (g, r, h, 1 - s)
    x_dev = (g, 1 - r, h, s)
    z_devs = [(g, r, lax.rem(h + j, heads), s) for j in range(1, heads)]
    barrier = pltpu.get_barrier_semaphore()
    far_devs = [(g, r, lax.rem(h + j, heads), 1 - s) for j in range(1, heads)]
    for device in [core_dev, x_dev] + z_devs + far_devs:
        pl.semaphore_signal(
            barrier, inc=1, device_id=device, device_id_type=pl.DeviceIdType.MESH
        )

    def remote(src, dst, send_sem, recv_sem, device):
        return pltpu.make_async_remote_copy(
            src_ref=src,
            dst_ref=dst,
            send_sem=send_sem,
            recv_sem=recv_sem,
            device_id=device,
            device_id_type=pl.DeviceIdType.MESH,
        )

    tokens = kv_ref.shape[0]
    new_rows = q_ref.shape[0]
    blocks = bt_ref.shape[1]
    block_len = tokens // blocks
    lane_t = lax.broadcasted_iota(jnp.int32, (1, tokens), 1)
    stored = lane_t // block_len
    place = jnp.zeros((1, tokens), jnp.int32)
    for i in range(blocks):
        place = jnp.where(stored == bt_ref[0, i], i, place)
    key_pos = place * block_len + lane_t % block_len - (len_ref[0] - new_rows)
    row_pos = lax.broadcasted_iota(jnp.int32, (2 * new_rows, 1), 0) % new_rows
    visible = key_pos <= row_pos
    lane_q = lax.broadcasted_iota(jnp.int32, (new_rows, 128), 1)
    low = lane_q < 64
    for pair in range(q_ref.shape[1] // 128):
        both = q_ref[:, pair * 128 : (pair + 1) * 128].astype(f32) * 0.125
        even = jnp.where(low, both, 0.0)
        odd = jnp.where(low, pltpu.roll(both, 64, axis=1), 0.0)
        stacked = jnp.concatenate([even, odd], axis=0).astype(bf16)
        scores = dot_rows(stacked, kv_ref[...])
        scores = jnp.where(visible, scores, MASKED)
        top = jnp.max(scores, axis=-1, keepdims=True)
        weights = jnp.exp(scores - top)
        total = jnp.sum(weights, axis=-1, keepdims=True)
        mixed = jnp.dot(weights.astype(bf16), kv_ref[...], preferred_element_type=f32) / total
        joined = jnp.where(low, pltpu.roll(mixed[:new_rows], 64, axis=1), mixed[new_rows:])
        attn[:, :, :, pair * 128 : (pair + 1) * 128] = joined.astype(bf16).reshape(
            heads, 2, share, 128
        )

    inner = attn.shape[3]
    psend[...] = dot_rows(attn[:, 1 - s].reshape(heads * share, inner), wo_ref[...]).astype(bf16)
    pl.semaphore_wait(barrier, 2 * heads)
    pair_copy = remote(psend, precv, core_send.at[0], core_recv.at[0], core_dev)
    pair_copy.start()
    pown[...] = dot_rows(attn[:, s].reshape(heads * share, inner), wo_ref[...]).reshape(
        heads, share, depth
    )
    pair_copy.wait_recv()
    pown[...] = pown[...] + precv[...].reshape(heads, share, depth).astype(f32)
    zsend[...] = pown[...].astype(bf16)
    order = sorted(range(1, heads), key=lambda j: -min(j, heads - j))
    z_copies = {}
    for j in order:
        z_copies[j] = remote(
            zsend.at[lax.rem(h + j, heads)],
            zrecv.at[j - 1],
            z_send.at[j - 1],
            z_recv.at[j - 1],
            z_devs[j - 1],
        )
        z_copies[j].start()
    sent = [pair_copy] + list(z_copies.values())

    slots = 2 * heads * cap
    slot = lax.broadcasted_iota(jnp.int32, (slots, share), 0)
    named = jnp.zeros((slots, share), f32)
    routed = jnp.zeros((slots, share), f32)
    for k in range(ids_ref.shape[0]):
        hit = ids_ref[k : k + 1, :] == slot // cap
        named = named + jnp.where(hit, 1.0, 0.0)
        routed = routed + jnp.where(hit, rw_ref[k : k + 1, :], 0.0)
    earlier = lax.broadcasted_iota(jnp.int32, (share, share), 0) < lax.broadcasted_iota(
        jnp.int32, (share, share), 1
    )
    rank = jnp.dot(
        named.astype(bf16), jnp.where(earlier, 1.0, 0.0).astype(bf16), preferred_element_type=f32
    )
    rank_here = jnp.where(rank == (slot % cap).astype(f32), 1.0, 0.0)
    pick = (named * rank_here).astype(bf16)
    mix = (routed * rank_here).T
    mix_coarse = mix.astype(bf16)
    mix_fine = (mix - mix_coarse.astype(f32)).astype(bf16)

    gathered = res_ref[...].astype(f32) + pown[h]
    for j in range(1, heads):
        z_copies[j].wait_recv()
        gathered = gathered + zrecv[j - 1].astype(f32)
    residual = gathered.astype(bf16)
    resid[...] = residual
    wide = residual.astype(f32)
    mean_square = jnp.mean(wide * wide, axis=-1, keepdims=True)
    normed = (wide * lax.rsqrt(mean_square + EPSILON) * gain_ref[...][None, :]).astype(bf16)
    disp[...] = (
        jnp.dot(pick, normed, preferred_element_type=f32)
        .astype(bf16)
        .reshape(heads, 2, cap, depth)
    )
    xin[r, h, s] = disp[h, s]

    def peer(j, other):
        return lax.rem(h + j, heads), (1 - s if other else s)

    def source(j, other):
        return lax.rem(h - j + heads, heads), (1 - s if other else s)

    near_first = order[::-1]
    routes = [(0, 1)] + [(j, other) for j in near_first for other in (0, 1)]
    routed_copies = {}
    for j, other in routes:
        to_h, to_s = peer(j, other)
        sem = heads - 1 + 2 * j + other
        routed_copies[j, other] = remote(
            disp.at[to_h, to_s],
            xin.at[r, h, s],
            z_send.at[sem],
            z_recv.at[sem],
            (g, r, to_h, to_s),
        )
        routed_copies[j, other].start()
    across = {}
    for j, other in [(0, 0)] + routes:
        if (j, other) != (0, 0):
            routed_copies[j, other].wait_recv()
        from_h, from_s = source(j, other)
        block = xin.at[r, from_h, from_s]
        sem = 2 * j + other
        across[j, other] = remote(block, block, x_send.at[sem], x_recv.at[sem], x_dev)
        across[j, other].start()
    for copy in across.values():
        copy.wait_recv()
    sent += list(routed_copies.values()) + list(across.values())

    rows_in = 4 * heads * cap
    weight_copies[0].wait()
    weight_copies[1].wait()

    def hidden_tile(tile):
        gate_out = dot_rows(xin[...].reshape(rows_in, depth), wg[tile, :])
        up_out = dot_rows(xin[...].reshape(rows_in, depth), wu[tile, :])
        act[:, tile] = (gate_out * jax.nn.sigmoid(1.702 * gate_out) * (up_out + 1.0)).astype(bf16)

    hidden = wg.shape[0]
    full = hidden // 256

    @pl.loop(0, full)
    def _(i):
        hidden_tile(pl.ds(pl.multiple_of(i * 256, 256), 256))

    if hidden % 256:
        hidden_tile(pl.ds(full * 256, hidden % 256))
    weight_copies[2].wait()

    count = len(chunks)
    per = len(chunk_refs) // count
    base_x, base_z = 2 * heads, 3 * heads - 1
    x_copies, line_copies = {}, {}
    back = [(j, other) for j in order for other in (0, 1)] + [(0, 1)]

    def multiply(c):
        cown, xsend, xrecv, back_send, back_recv = chunk_refs[c * per : (c + 1) * per]
        start, width = chunks[c]
        cown[...] = jnp.dot(
            act[...], wd[:, start : start + width], preferred_element_type=f32
        ).reshape(2, heads, 2, cap, width)
        xsend[...] = cown[1 - r].astype(bf16)
        x_copies[c] = remote(xsend, xrecv, x_send.at[base_x + c], x_recv.at[base_x + c], x_dev)
        x_copies[c].start()

    def over_req(c):
        cown, xsend, xrecv, back_send, back_recv = chunk_refs[c * per : (c + 1) * per]
        x_copies[c].wait_recv()
        back_send[...] = (cown[r].astype(bf16).astype(f32) + xrecv[...].astype(f32)).astype(bf16)
        line_copies[c] = {}
        for j, other in back:
            to_h, to_s = peer(j, other)
            sem = base_z + c * 2 * heads + 2 * j + other
            line_copies[c][j, other] = remote(
                back_send.at[to_h, to_s],
                back_recv.at[h, s],
                z_send.at[sem],
                z_recv.at[sem],
                (g, r, to_h, to_s),
            )
            line_copies[c][j, other].start()
        back_recv[h, s] = back_send[h, s]

    def at_rows(c):
        cown, xsend, xrecv, back_send, back_recv = chunk_refs[c * per : (c + 1) * per]
        start, width = chunks[c]
        for copy in line_copies[c].values():
            copy.wait_recv()
        outs = back_recv[...].reshape(slots, width)
        total = jnp.dot(mix_coarse, outs, preferred_element_type=f32)
        total = total + jnp.dot(mix_fine, outs, preferred_element_type=f32)
        total = total + resid[:, start : start + width].astype(f32)
        out_ref[:, start : start + width] = total.astype(bf16)

    for step in range(count + 2):
        for lag, stage in enumerate((multiply, over_req, at_rows)):
            if 0 <= step - lag < count:
                stage(step - lag)
    sent += list(x_copies.values())
    for copies in line_copies.values():
        sent += list(copies.values())
    for copy in sent:
        copy.wait_send()


def fused_on_device(
    queries,
    cache_pool,
    lengths,
    block_table,
    out_proj,
    residual_in,
    norm_gain,
    expert_ids,
    route_weight,
    gate_weight,
    up_weight,
    down_weight,
):
    bf16, f32 = jnp.bfloat16, jnp.float32
    heads = lax.axis_size("head")
    share, depth = residual_in.shape
    inner = queries.shape[1]
    hidden = gate_weight.shape[2]
    cap = share * TOP // (heads * 2)
    tokens = cache_pool.shape[0] * cache_pool.shape[1]
    kv = lax.dynamic_index_in_dim(cache_pool, lax.axis_index("sec"), axis=2, keepdims=False)
    kv = kv.reshape(tokens, cache_pool.shape[3])
    chunks = lane_chunks(depth, CHUNK)
    count = len(chunks)
    vmem = pltpu.VMEM
    scratch = [
        vmem((hidden, depth), bf16),
        vmem((hidden, depth), bf16),
        vmem((hidden, depth), bf16),
        vmem((heads, 2, share, inner), bf16),
        vmem((heads * share, depth), bf16),
        vmem((heads * share, depth), bf16),
        vmem((heads, share, depth), f32),
        vmem((heads, share, depth), bf16),
        vmem((heads - 1, share, depth), bf16),
        vmem((share, depth), bf16),
        vmem((heads, 2, cap, depth), bf16),
        vmem((2, heads, 2, cap, depth), bf16),
        vmem((4 * heads * cap, hidden), bf16),
        pltpu.SemaphoreType.DMA((3,)),
        pltpu.SemaphoreType.DMA((1,)),
        pltpu.SemaphoreType.DMA((1,)),
        pltpu.SemaphoreType.DMA((2 * heads + count,)),
        pltpu.SemaphoreType.DMA((2 * heads + count,)),
        pltpu.SemaphoreType.DMA((heads - 1 + 2 * heads * (1 + count),)),
        pltpu.SemaphoreType.DMA((heads - 1 + 2 * heads * (1 + count),)),
    ]
    for start, width in chunks:
        scratch += [
            vmem((2, heads, 2, cap, width), f32),
            vmem((heads, 2, cap, width), bf16),
            vmem((heads, 2, cap, width), bf16),
            vmem((heads, 2, cap, width), bf16),
            vmem((heads, 2, cap, width), bf16),
        ]
    in_vmem = pl.BlockSpec(memory_space=pltpu.VMEM)
    in_smem = pl.BlockSpec(memory_space=pltpu.SMEM)
    in_place = pl.BlockSpec(memory_space=pl.ANY)
    return pl.pallas_call(
        functools.partial(layer_kernel, chunks),
        out_shape=jax.ShapeDtypeStruct((share, depth), bf16),
        in_specs=[in_vmem, in_vmem, in_smem, in_smem] + [in_vmem] * 5 + [in_place] * 3,
        out_specs=in_vmem,
        scratch_shapes=scratch,
        compiler_params=pltpu.CompilerParams(
            collective_id=0, has_side_effects=True, vmem_limit_bytes=58 << 20
        ),
    )(
        queries,
        kv,
        lengths,
        block_table,
        out_proj.T,
        residual_in,
        norm_gain,
        expert_ids.T,
        route_weight.T,
        jnp.swapaxes(gate_weight, 1, 2),
        jnp.swapaxes(up_weight, 1, 2),
        down_weight,
    )


def solution(mesh):
    sizes = dict(mesh.shape)
    fused = sizes["req"] == 2 and sizes["sec"] == 2 and sizes["head"] == 4
    return jax.shard_map(
        fused_on_device if fused else on_device,
        mesh=mesh,
        in_specs=(
            P(("groups", "req"), ("head", "sec")),
            P(("groups", "req"), None, "head", None),
            P(("groups", "req")),
            P(("groups", "req"), None),
            P(("head", "sec"), None),
            P(("groups", "req", "head", "sec"), None),
            P(),
            P(("groups", "req", "head", "sec"), None),
            P(("groups", "req", "head", "sec"), None),
            P(("head", "sec"), None, "req"),
            P(("head", "sec"), None, "req"),
            P(("head", "sec"), "req", None),
        ),
        out_specs=P(("groups", "req", "head", "sec"), None),
        check_vma=False,
    )
```

```python
import functools
import math

import jax
import jax.numpy as jnp
from jax import lax
from jax.experimental import pallas as pl
from jax.experimental.pallas import tpu as pltpu
from jax.sharding import PartitionSpec as P

QH = 64
KVH = 8
TOP = 4


EPSILON = 1e-05
MASKED = -1e30
CHUNK = 768


def run_expert(row_block, gate_weight, up_weight, down_weight):
    row_shape = row_block.shape
    flat_rows = row_block.reshape(-1, row_shape[-1])
    gate_out = jnp.dot(flat_rows, gate_weight[0], preferred_element_type=jnp.float32)
    up_out = jnp.dot(flat_rows, up_weight[0], preferred_element_type=jnp.float32)
    activated = (gate_out * jax.nn.sigmoid(1.702 * gate_out) * (up_out + 1.0)).astype(jnp.bfloat16)
    partial_value = jnp.dot(activated, down_weight[0], preferred_element_type=jnp.float32)
    return partial_value.astype(jnp.bfloat16).reshape(row_shape[:-1] + (partial_value.shape[-1],))


def masked_scores(query_heads, key_block, positions, score_scale):
    scores = (
        jnp.einsum("nhd,thd->hnt", query_heads, key_block, preferred_element_type=jnp.float32)
        * score_scale
    )
    key_positions = jnp.arange(key_block.shape[0], dtype=jnp.int32)
    visible = key_positions[None, None, :] <= positions[None, :, None]
    return jnp.where(visible, scores, MASKED)


def on_device(
    queries,
    cache_pool,
    lengths,
    block_table,
    out_proj,
    residual_in,
    norm_gain,
    expert_ids,
    route_weight,
    gate_weight,
    up_weight,
    down_weight,
):
    head_dim = cache_pool.shape[3] // 2
    block_len = cache_pool.shape[1]
    max_blocks = cache_pool.shape[0]
    new_rows = queries.shape[0]
    local_heads = queries.shape[1] // head_dim
    score_scale = 1.0 / math.sqrt(head_dim)
    context = lengths[0]
    sequence = cache_pool[block_table[0]]
    kv_choice = (
        lax.axis_index("sec") * local_heads + jnp.arange(local_heads, dtype=jnp.int32)
    ) // (QH // KVH)
    selected = jnp.take(sequence, kv_choice, axis=2)
    key_heads = selected[..., :head_dim]
    value_heads = selected[..., head_dim:]
    query_heads = queries.reshape(new_rows, local_heads, head_dim)
    positions = context - new_rows + jnp.arange(new_rows, dtype=jnp.int32)
    all_keys = key_heads.reshape(max_blocks * block_len, local_heads, head_dim)
    all_values = value_heads.reshape(max_blocks * block_len, local_heads, head_dim)
    scores = masked_scores(query_heads, all_keys, positions, score_scale)
    row_max = jnp.max(scores, axis=-1, keepdims=True)
    exp_scores = jnp.exp(scores - row_max)
    row_sum = jnp.sum(exp_scores, axis=-1, keepdims=True)
    probabilities = (exp_scores / row_sum).astype(jnp.bfloat16)
    attended = jnp.einsum(
        "hnt,thd->nhd", probabilities, all_values, preferred_element_type=jnp.float32
    )
    attn = attended.astype(jnp.bfloat16).reshape(new_rows, local_heads * head_dim)
    share_rows = new_rows // (lax.axis_size("head") * lax.axis_size("sec"))
    partial_value = jnp.dot(attn, out_proj, preferred_element_type=jnp.float32)
    projected = lax.psum_scatter(
        partial_value.astype(jnp.bfloat16).astype(jnp.float32).astype(jnp.bfloat16),
        ("head", "sec"),
        scatter_dimension=0,
        tiled=True,
    ).astype(jnp.float32)
    residual = (residual_in.astype(jnp.float32) + projected).astype(jnp.bfloat16)
    residual_wide = residual.astype(jnp.float32)
    mean_square = jnp.mean(residual_wide * residual_wide, axis=-1, keepdims=True)
    normed = (residual_wide * lax.rsqrt(mean_square + EPSILON) * norm_gain).astype(jnp.bfloat16)
    experts_all = lax.axis_size("head") * lax.axis_size("sec")
    capacity = share_rows * TOP // experts_all
    flat_ids = expert_ids.reshape(-1)
    onehot = (flat_ids[:, None] == jnp.arange(experts_all, dtype=jnp.int32)[None, :]).astype(
        jnp.int32
    )
    before = jnp.cumsum(onehot, axis=0) - onehot
    target = flat_ids * capacity + jnp.sum(before * onehot, axis=1)
    source_row = (
        jnp.zeros((experts_all * capacity,), jnp.int32)
        .at[target]
        .set(jnp.arange(share_rows * TOP, dtype=jnp.int32) // TOP)
    )
    buffer = normed[source_row].reshape(experts_all, capacity, normed.shape[1])
    copies = lax.all_gather(buffer[None], "req", axis=0, tiled=True)
    results = run_expert(
        lax.all_to_all(copies, ("head", "sec"), split_axis=1, concat_axis=1, tiled=True),
        gate_weight,
        up_weight,
        down_weight,
    )
    partial_back = lax.all_to_all(results, ("head", "sec"), split_axis=1, concat_axis=1, tiled=True)
    returned = (
        lax.psum_scatter(
            partial_back.astype(jnp.float32).astype(jnp.bfloat16),
            "req",
            scatter_dimension=0,
            tiled=True,
        )
        .astype(jnp.float32)[0]
        .astype(jnp.bfloat16)
    )
    gathered_out = returned.reshape(experts_all * capacity, -1)[target].reshape(share_rows, TOP, -1)
    expert_mix = jnp.sum(route_weight[:, :, None] * gathered_out.astype(jnp.float32), axis=1)
    return (residual.astype(jnp.float32) + expert_mix).astype(jnp.bfloat16)


def lane_chunks(width, size):
    return [(start, min(size, width - start)) for start in range(0, width, size)]


def dot_rows(rows, weight_rows):
    return lax.dot_general(
        rows, weight_rows, (((1,), (1,)), ((), ())), preferred_element_type=jnp.float32
    )


def layer_kernel(
    chunks,
    q_ref,
    kv_ref,
    len_ref,
    bt_ref,
    wo_ref,
    res_ref,
    gain_ref,
    ids_ref,
    rw_ref,
    wg_hbm,
    wu_hbm,
    wd_hbm,
    out_ref,
    wg,
    wu,
    wd,
    attn,
    psend,
    precv,
    pown,
    zsend,
    zrecv,
    resid,
    disp,
    zin,
    xin,
    act,
    w_sem,
    core_send,
    core_recv,
    x_send,
    x_recv,
    z_send,
    z_recv,
    *chunk_refs,
):
    g, r = lax.axis_index("groups"), lax.axis_index("req")
    h, s = lax.axis_index("head"), lax.axis_index("sec")
    heads = attn.shape[0]
    share = attn.shape[2]
    depth = res_ref.shape[1]
    cap = disp.shape[2]
    f32, bf16 = jnp.float32, jnp.bfloat16

    weight_copies = [
        pltpu.make_async_copy(src.at[0], dst, w_sem.at[i])
        for i, (src, dst) in enumerate(((wg_hbm, wg), (wu_hbm, wu), (wd_hbm, wd)))
    ]
    for copy in weight_copies:
        copy.start()

    core_dev = (g, r, h, 1 - s)
    x_dev = (g, 1 - r, h, s)
    z_devs = [(g, r, lax.rem(h + j, heads), s) for j in range(1, heads)]
    barrier = pltpu.get_barrier_semaphore()
    for device in [core_dev, x_dev] + z_devs:
        pl.semaphore_signal(
            barrier, inc=1, device_id=device, device_id_type=pl.DeviceIdType.MESH
        )

    def remote(src, dst, send_sem, recv_sem, device):
        return pltpu.make_async_remote_copy(
            src_ref=src,
            dst_ref=dst,
            send_sem=send_sem,
            recv_sem=recv_sem,
            device_id=device,
            device_id_type=pl.DeviceIdType.MESH,
        )

    tokens = kv_ref.shape[0]
    new_rows = q_ref.shape[0]
    blocks = bt_ref.shape[1]
    block_len = tokens // blocks
    lane_t = lax.broadcasted_iota(jnp.int32, (1, tokens), 1)
    stored = lane_t // block_len
    place = jnp.zeros((1, tokens), jnp.int32)
    for i in range(blocks):
        place = jnp.where(stored == bt_ref[0, i], i, place)
    key_pos = place * block_len + lane_t % block_len - (len_ref[0] - new_rows)
    row_pos = lax.broadcasted_iota(jnp.int32, (2 * new_rows, 1), 0) % new_rows
    visible = key_pos <= row_pos
    lane_q = lax.broadcasted_iota(jnp.int32, (new_rows, 128), 1)
    low = lane_q < 64
    for pair in range(q_ref.shape[1] // 128):
        both = q_ref[:, pair * 128 : (pair + 1) * 128].astype(f32) * 0.125
        even = jnp.where(low, both, 0.0)
        odd = jnp.where(low, pltpu.roll(both, 64, axis=1), 0.0)
        stacked = jnp.concatenate([even, odd], axis=0).astype(bf16)
        scores = dot_rows(stacked, kv_ref[...])
        scores = jnp.where(visible, scores, MASKED)
        top = jnp.max(scores, axis=-1, keepdims=True)
        weights = jnp.exp(scores - top)
        total = jnp.sum(weights, axis=-1, keepdims=True)
        mixed = jnp.dot(weights.astype(bf16), kv_ref[...], preferred_element_type=f32) / total
        joined = jnp.where(low, pltpu.roll(mixed[:new_rows], 64, axis=1), mixed[new_rows:])
        attn[:, :, :, pair * 128 : (pair + 1) * 128] = joined.astype(bf16).reshape(
            heads, 2, share, 128
        )

    inner = attn.shape[3]
    psend[...] = dot_rows(attn[:, 1 - s].reshape(heads * share, inner), wo_ref[...]).astype(bf16)
    pl.semaphore_wait(barrier, 1 + heads)
    pair_copy = remote(psend, precv, core_send.at[0], core_recv.at[0], core_dev)
    pair_copy.start()
    pown[...] = dot_rows(attn[:, s].reshape(heads * share, inner), wo_ref[...]).reshape(
        heads, share, depth
    )
    pair_copy.wait_recv()
    pown[...] = pown[...] + precv[...].reshape(heads, share, depth).astype(f32)
    zsend[...] = pown[...].astype(bf16)
    order = sorted(range(1, heads), key=lambda j: -min(j, heads - j))
    z_copies = {}
    for j in order:
        z_copies[j] = remote(
            zsend.at[lax.rem(h + j, heads)],
            zrecv.at[j - 1],
            z_send.at[j - 1],
            z_recv.at[j - 1],
            z_devs[j - 1],
        )
        z_copies[j].start()
    sent = [pair_copy] + list(z_copies.values())

    slots = 2 * heads * cap
    slot = lax.broadcasted_iota(jnp.int32, (slots, share), 0)
    named = jnp.zeros((slots, share), f32)
    routed = jnp.zeros((slots, share), f32)
    for k in range(ids_ref.shape[0]):
        hit = ids_ref[k : k + 1, :] == slot // cap
        named = named + jnp.where(hit, 1.0, 0.0)
        routed = routed + jnp.where(hit, rw_ref[k : k + 1, :], 0.0)
    earlier = lax.broadcasted_iota(jnp.int32, (share, share), 0) < lax.broadcasted_iota(
        jnp.int32, (share, share), 1
    )
    rank = jnp.dot(
        named.astype(bf16), jnp.where(earlier, 1.0, 0.0).astype(bf16), preferred_element_type=f32
    )
    rank_here = jnp.where(rank == (slot % cap).astype(f32), 1.0, 0.0)
    pick = (named * rank_here).astype(bf16)
    mix = (routed * rank_here).T
    mix_coarse = mix.astype(bf16)
    mix_fine = (mix - mix_coarse.astype(f32)).astype(bf16)

    gathered = res_ref[...].astype(f32) + pown[h]
    for j in range(1, heads):
        z_copies[j].wait_recv()
        gathered = gathered + zrecv[j - 1].astype(f32)
    residual = gathered.astype(bf16)
    resid[...] = residual
    wide = residual.astype(f32)
    mean_square = jnp.mean(wide * wide, axis=-1, keepdims=True)
    normed = (wide * lax.rsqrt(mean_square + EPSILON) * gain_ref[...][None, :]).astype(bf16)
    disp[...] = (
        jnp.dot(pick, normed, preferred_element_type=f32)
        .astype(bf16)
        .reshape(heads, 2, cap, depth)
    )
    zin[h] = disp[h]

    near_first = order[::-1]
    line_in, to_core, across = {}, {}, {}
    for j in near_first:
        sem = heads - 2 + j
        line_in[j] = remote(
            disp.at[lax.rem(h + j, heads)],
            zin.at[h],
            z_send.at[sem],
            z_recv.at[sem],
            z_devs[j - 1],
        )
        line_in[j].start()

    def cross(j, core):
        block = xin.at[r, lax.rem(h - j + heads, heads), core]
        sem = 2 * j + (0 if core is s else 1)
        across[sem] = remote(block, block, x_send.at[sem], x_recv.at[sem], x_dev)
        across[sem].start()

    for j in [0] + near_first:
        if j:
            line_in[j].wait_recv()
        origin = lax.rem(h - j + heads, heads)
        to_core[j] = remote(
            zin.at[origin, 1 - s],
            xin.at[r, origin, s],
            core_send.at[1 + j],
            core_recv.at[1 + j],
            core_dev,
        )
        to_core[j].start()
        xin[r, origin, s] = zin[origin, s]
        cross(j, s)
        to_core[j].wait_recv()
        cross(j, 1 - s)
    for copy in across.values():
        copy.wait_recv()
    sent += list(line_in.values()) + list(to_core.values()) + list(across.values())

    rows_in = 4 * heads * cap
    weight_copies[0].wait()
    weight_copies[1].wait()

    def hidden_tile(tile):
        gate_out = dot_rows(xin[...].reshape(rows_in, depth), wg[tile, :])
        up_out = dot_rows(xin[...].reshape(rows_in, depth), wu[tile, :])
        act[:, tile] = (gate_out * jax.nn.sigmoid(1.702 * gate_out) * (up_out + 1.0)).astype(bf16)

    hidden = wg.shape[0]
    full = hidden // 256

    @pl.loop(0, full)
    def _(i):
        hidden_tile(pl.ds(pl.multiple_of(i * 256, 256), 256))

    if hidden % 256:
        hidden_tile(pl.ds(full * 256, hidden % 256))
    weight_copies[2].wait()

    count = len(chunks)
    per = len(chunk_refs) // count
    base_core, base_x, base_z = 1 + heads, 2 * heads, 2 * (heads - 1)
    x_copies, core_copies, line_copies = {}, {}, {}

    def multiply(c):
        cown, xsend, xrecv, to_other, back_send, back_recv = chunk_refs[c * per : (c + 1) * per]
        start, width = chunks[c]
        cown[...] = jnp.dot(
            act[...], wd[:, start : start + width], preferred_element_type=f32
        ).reshape(2, heads, 2, cap, width)
        xsend[...] = cown[1 - r].astype(bf16)
        x_copies[c] = remote(xsend, xrecv, x_send.at[base_x + c], x_recv.at[base_x + c], x_dev)
        x_copies[c].start()

    def over_req(c):
        cown, xsend, xrecv, to_other, back_send, back_recv = chunk_refs[c * per : (c + 1) * per]
        x_copies[c].wait_recv()
        to_other[...] = (cown[r].astype(bf16).astype(f32) + xrecv[...].astype(f32)).astype(bf16)
        core_copies[c] = remote(
            to_other.at[:, 1 - s],
            back_send.at[:, s],
            core_send.at[base_core + c],
            core_recv.at[base_core + c],
            core_dev,
        )
        core_copies[c].start()
        back_send[:, s] = to_other[:, s]

    def along_line(c):
        cown, xsend, xrecv, to_other, back_send, back_recv = chunk_refs[c * per : (c + 1) * per]
        core_copies[c].wait_recv()
        line_copies[c] = {}
        for j in order:
            sem = base_z + c * (heads - 1) + j - 1
            line_copies[c][j] = remote(
                back_send.at[lax.rem(h + j, heads)],
                back_recv.at[h],
                z_send.at[sem],
                z_recv.at[sem],
                z_devs[j - 1],
            )
            line_copies[c][j].start()
        back_recv[h] = back_send[h]

    def at_rows(c):
        cown, xsend, xrecv, to_other, back_send, back_recv = chunk_refs[c * per : (c + 1) * per]
        start, width = chunks[c]
        for copy in line_copies[c].values():
            copy.wait_recv()
        outs = back_recv[...].reshape(slots, width)
        total = jnp.dot(mix_coarse, outs, preferred_element_type=f32)
        total = total + jnp.dot(mix_fine, outs, preferred_element_type=f32)
        total = total + resid[:, start : start + width].astype(f32)
        out_ref[:, start : start + width] = total.astype(bf16)

    for c in range(count):
        multiply(c)
    for step in range(count + 1):
        for lag, stage in enumerate((over_req, along_line)):
            if 0 <= step - lag < count:
                stage(step - lag)
    for c in range(count):
        at_rows(c)
    sent += list(x_copies.values()) + list(core_copies.values())
    for copies in line_copies.values():
        sent += list(copies.values())
    for copy in sent:
        copy.wait_send()


def fused_on_device(
    queries,
    cache_pool,
    lengths,
    block_table,
    out_proj,
    residual_in,
    norm_gain,
    expert_ids,
    route_weight,
    gate_weight,
    up_weight,
    down_weight,
):
    bf16, f32 = jnp.bfloat16, jnp.float32
    heads = lax.axis_size("head")
    share, depth = residual_in.shape
    inner = queries.shape[1]
    hidden = gate_weight.shape[2]
    cap = share * TOP // (heads * 2)
    tokens = cache_pool.shape[0] * cache_pool.shape[1]
    kv = lax.dynamic_index_in_dim(cache_pool, lax.axis_index("sec"), axis=2, keepdims=False)
    kv = kv.reshape(tokens, cache_pool.shape[3])
    chunks = lane_chunks(depth, CHUNK)
    count = len(chunks)
    vmem = pltpu.VMEM
    scratch = [
        vmem((hidden, depth), bf16),
        vmem((hidden, depth), bf16),
        vmem((hidden, depth), bf16),
        vmem((heads, 2, share, inner), bf16),
        vmem((heads * share, depth), bf16),
        vmem((heads * share, depth), bf16),
        vmem((heads, share, depth), f32),
        vmem((heads, share, depth), bf16),
        vmem((heads - 1, share, depth), bf16),
        vmem((share, depth), bf16),
        vmem((heads, 2, cap, depth), bf16),
        vmem((heads, 2, cap, depth), bf16),
        vmem((2, heads, 2, cap, depth), bf16),
        vmem((4 * heads * cap, hidden), bf16),
        pltpu.SemaphoreType.DMA((3,)),
        pltpu.SemaphoreType.DMA((1 + heads + count,)),
        pltpu.SemaphoreType.DMA((1 + heads + count,)),
        pltpu.SemaphoreType.DMA((2 * heads + count,)),
        pltpu.SemaphoreType.DMA((2 * heads + count,)),
        pltpu.SemaphoreType.DMA(((heads - 1) * (2 + count),)),
        pltpu.SemaphoreType.DMA(((heads - 1) * (2 + count),)),
    ]
    for start, width in chunks:
        scratch += [
            vmem((2, heads, 2, cap, width), f32),
            vmem((heads, 2, cap, width), bf16),
            vmem((heads, 2, cap, width), bf16),
            vmem((heads, 2, cap, width), bf16),
            vmem((heads, 2, cap, width), bf16),
            vmem((heads, 2, cap, width), bf16),
        ]
    in_vmem = pl.BlockSpec(memory_space=pltpu.VMEM)
    in_smem = pl.BlockSpec(memory_space=pltpu.SMEM)
    in_place = pl.BlockSpec(memory_space=pl.ANY)
    return pl.pallas_call(
        functools.partial(layer_kernel, chunks),
        out_shape=jax.ShapeDtypeStruct((share, depth), bf16),
        in_specs=[in_vmem, in_vmem, in_smem, in_smem] + [in_vmem] * 5 + [in_place] * 3,
        out_specs=in_vmem,
        scratch_shapes=scratch,
        compiler_params=pltpu.CompilerParams(
            collective_id=0, has_side_effects=True, vmem_limit_bytes=58 << 20
        ),
    )(
        queries,
        kv,
        lengths,
        block_table,
        out_proj.T,
        residual_in,
        norm_gain,
        expert_ids.T,
        route_weight.T,
        jnp.swapaxes(gate_weight, 1, 2),
        jnp.swapaxes(up_weight, 1, 2),
        down_weight,
    )


def solution(mesh):
    sizes = dict(mesh.shape)
    fused = sizes["req"] == 2 and sizes["sec"] == 2 and sizes["head"] == 4
    return jax.shard_map(
        fused_on_device if fused else on_device,
        mesh=mesh,
        in_specs=(
            P(("groups", "req"), ("head", "sec")),
            P(("groups", "req"), None, "head", None),
            P(("groups", "req")),
            P(("groups", "req"), None),
            P(("head", "sec"), None),
            P(("groups", "req", "head", "sec"), None),
            P(),
            P(("groups", "req", "head", "sec"), None),
            P(("groups", "req", "head", "sec"), None),
            P(("head", "sec"), None, "req"),
            P(("head", "sec"), None, "req"),
            P(("head", "sec"), "req", None),
        ),
        out_specs=P(("groups", "req", "head", "sec"), None),
        check_vma=False,
    )
```

```python
import functools
import math

import jax
import jax.numpy as jnp
from jax import lax
from jax.experimental import pallas as pl
from jax.experimental.pallas import tpu as pltpu
from jax.sharding import PartitionSpec as P

QH = 64
KVH = 8
TOP = 4


EPSILON = 1e-05
MASKED = -1e30
CHUNK = 512


def run_expert(row_block, gate_weight, up_weight, down_weight):
    row_shape = row_block.shape
    flat_rows = row_block.reshape(-1, row_shape[-1])
    gate_out = jnp.dot(flat_rows, gate_weight[0], preferred_element_type=jnp.float32)
    up_out = jnp.dot(flat_rows, up_weight[0], preferred_element_type=jnp.float32)
    activated = (gate_out * jax.nn.sigmoid(1.702 * gate_out) * (up_out + 1.0)).astype(jnp.bfloat16)
    partial_value = jnp.dot(activated, down_weight[0], preferred_element_type=jnp.float32)
    return partial_value.astype(jnp.bfloat16).reshape(row_shape[:-1] + (partial_value.shape[-1],))


def masked_scores(query_heads, key_block, positions, score_scale):
    scores = (
        jnp.einsum("nhd,thd->hnt", query_heads, key_block, preferred_element_type=jnp.float32)
        * score_scale
    )
    key_positions = jnp.arange(key_block.shape[0], dtype=jnp.int32)
    visible = key_positions[None, None, :] <= positions[None, :, None]
    return jnp.where(visible, scores, MASKED)


def on_device(
    queries,
    cache_pool,
    lengths,
    block_table,
    out_proj,
    residual_in,
    norm_gain,
    expert_ids,
    route_weight,
    gate_weight,
    up_weight,
    down_weight,
):
    head_dim = cache_pool.shape[3] // 2
    block_len = cache_pool.shape[1]
    max_blocks = cache_pool.shape[0]
    new_rows = queries.shape[0]
    local_heads = queries.shape[1] // head_dim
    score_scale = 1.0 / math.sqrt(head_dim)
    context = lengths[0]
    sequence = cache_pool[block_table[0]]
    kv_choice = (
        lax.axis_index("sec") * local_heads + jnp.arange(local_heads, dtype=jnp.int32)
    ) // (QH // KVH)
    selected = jnp.take(sequence, kv_choice, axis=2)
    key_heads = selected[..., :head_dim]
    value_heads = selected[..., head_dim:]
    query_heads = queries.reshape(new_rows, local_heads, head_dim)
    positions = context - new_rows + jnp.arange(new_rows, dtype=jnp.int32)
    all_keys = key_heads.reshape(max_blocks * block_len, local_heads, head_dim)
    all_values = value_heads.reshape(max_blocks * block_len, local_heads, head_dim)
    scores = masked_scores(query_heads, all_keys, positions, score_scale)
    row_max = jnp.max(scores, axis=-1, keepdims=True)
    exp_scores = jnp.exp(scores - row_max)
    row_sum = jnp.sum(exp_scores, axis=-1, keepdims=True)
    probabilities = (exp_scores / row_sum).astype(jnp.bfloat16)
    attended = jnp.einsum(
        "hnt,thd->nhd", probabilities, all_values, preferred_element_type=jnp.float32
    )
    attn = attended.astype(jnp.bfloat16).reshape(new_rows, local_heads * head_dim)
    share_rows = new_rows // (lax.axis_size("head") * lax.axis_size("sec"))
    partial_value = jnp.dot(attn, out_proj, preferred_element_type=jnp.float32)
    projected = lax.psum_scatter(
        partial_value.astype(jnp.bfloat16).astype(jnp.float32).astype(jnp.bfloat16),
        ("head", "sec"),
        scatter_dimension=0,
        tiled=True,
    ).astype(jnp.float32)
    residual = (residual_in.astype(jnp.float32) + projected).astype(jnp.bfloat16)
    residual_wide = residual.astype(jnp.float32)
    mean_square = jnp.mean(residual_wide * residual_wide, axis=-1, keepdims=True)
    normed = (residual_wide * lax.rsqrt(mean_square + EPSILON) * norm_gain).astype(jnp.bfloat16)
    experts_all = lax.axis_size("head") * lax.axis_size("sec")
    capacity = share_rows * TOP // experts_all
    flat_ids = expert_ids.reshape(-1)
    onehot = (flat_ids[:, None] == jnp.arange(experts_all, dtype=jnp.int32)[None, :]).astype(
        jnp.int32
    )
    before = jnp.cumsum(onehot, axis=0) - onehot
    target = flat_ids * capacity + jnp.sum(before * onehot, axis=1)
    source_row = (
        jnp.zeros((experts_all * capacity,), jnp.int32)
        .at[target]
        .set(jnp.arange(share_rows * TOP, dtype=jnp.int32) // TOP)
    )
    buffer = normed[source_row].reshape(experts_all, capacity, normed.shape[1])
    copies = lax.all_gather(buffer[None], "req", axis=0, tiled=True)
    results = run_expert(
        lax.all_to_all(copies, ("head", "sec"), split_axis=1, concat_axis=1, tiled=True),
        gate_weight,
        up_weight,
        down_weight,
    )
    partial_back = lax.all_to_all(results, ("head", "sec"), split_axis=1, concat_axis=1, tiled=True)
    returned = (
        lax.psum_scatter(
            partial_back.astype(jnp.float32).astype(jnp.bfloat16),
            "req",
            scatter_dimension=0,
            tiled=True,
        )
        .astype(jnp.float32)[0]
        .astype(jnp.bfloat16)
    )
    gathered_out = returned.reshape(experts_all * capacity, -1)[target].reshape(share_rows, TOP, -1)
    expert_mix = jnp.sum(route_weight[:, :, None] * gathered_out.astype(jnp.float32), axis=1)
    return (residual.astype(jnp.float32) + expert_mix).astype(jnp.bfloat16)


def lane_chunks(width, size):
    return [(start, min(size, width - start)) for start in range(0, width, size)]


def dot_rows(rows, weight_rows):
    return lax.dot_general(
        rows, weight_rows, (((1,), (1,)), ((), ())), preferred_element_type=jnp.float32
    )


def layer_kernel(
    chunks,
    q_ref,
    kv_ref,
    len_ref,
    bt_ref,
    wo_ref,
    res_ref,
    gain_ref,
    ids_ref,
    rw_ref,
    wg_hbm,
    wu_hbm,
    wd_hbm,
    out_ref,
    wg,
    wu,
    wd,
    attn,
    psend,
    precv,
    pown,
    zsend,
    zrecv,
    resid,
    disp,
    zin,
    xin,
    act,
    w_sem,
    core_send,
    core_recv,
    x_send,
    x_recv,
    z_send,
    z_recv,
    *chunk_refs,
):
    g, r = lax.axis_index("groups"), lax.axis_index("req")
    h, s = lax.axis_index("head"), lax.axis_index("sec")
    heads = attn.shape[0]
    share = attn.shape[2]
    depth = res_ref.shape[1]
    cap = disp.shape[2]
    f32, bf16 = jnp.float32, jnp.bfloat16

    weight_copies = [
        pltpu.make_async_copy(src.at[0], dst, w_sem.at[i])
        for i, (src, dst) in enumerate(((wg_hbm, wg), (wu_hbm, wu), (wd_hbm, wd)))
    ]
    for copy in weight_copies:
        copy.start()

    core_dev = (g, r, h, 1 - s)
    x_dev = (g, 1 - r, h, s)
    z_devs = [(g, r, lax.rem(h + j, heads), s) for j in range(1, heads)]
    barrier = pltpu.get_barrier_semaphore()
    for device in [core_dev, x_dev] + z_devs:
        pl.semaphore_signal(
            barrier, inc=1, device_id=device, device_id_type=pl.DeviceIdType.MESH
        )

    def remote(src, dst, send_sem, recv_sem, device):
        return pltpu.make_async_remote_copy(
            src_ref=src,
            dst_ref=dst,
            send_sem=send_sem,
            recv_sem=recv_sem,
            device_id=device,
            device_id_type=pl.DeviceIdType.MESH,
        )

    tokens = kv_ref.shape[0]
    new_rows = q_ref.shape[0]
    blocks = bt_ref.shape[1]
    block_len = tokens // blocks
    lane_t = lax.broadcasted_iota(jnp.int32, (1, tokens), 1)
    stored = lane_t // block_len
    place = jnp.zeros((1, tokens), jnp.int32)
    for i in range(blocks):
        place = jnp.where(stored == bt_ref[0, i], i, place)
    key_pos = place * block_len + lane_t % block_len - (len_ref[0] - new_rows)
    row_pos = lax.broadcasted_iota(jnp.int32, (2 * new_rows, 1), 0) % new_rows
    visible = key_pos <= row_pos
    lane_q = lax.broadcasted_iota(jnp.int32, (new_rows, 128), 1)
    low = lane_q < 64
    for pair in range(q_ref.shape[1] // 128):
        both = q_ref[:, pair * 128 : (pair + 1) * 128].astype(f32) * 0.125
        even = jnp.where(low, both, 0.0)
        odd = jnp.where(low, pltpu.roll(both, 64, axis=1), 0.0)
        stacked = jnp.concatenate([even, odd], axis=0).astype(bf16)
        scores = dot_rows(stacked, kv_ref[...])
        scores = jnp.where(visible, scores, MASKED)
        top = jnp.max(scores, axis=-1, keepdims=True)
        weights = jnp.exp(scores - top)
        total = jnp.sum(weights, axis=-1, keepdims=True)
        mixed = jnp.dot(weights.astype(bf16), kv_ref[...], preferred_element_type=f32) / total
        joined = jnp.where(low, pltpu.roll(mixed[:new_rows], 64, axis=1), mixed[new_rows:])
        attn[:, :, :, pair * 128 : (pair + 1) * 128] = joined.astype(bf16).reshape(
            heads, 2, share, 128
        )

    inner = attn.shape[3]
    psend[...] = dot_rows(attn[:, 1 - s].reshape(heads * share, inner), wo_ref[...]).astype(bf16)
    pl.semaphore_wait(barrier, 1 + heads)
    pair_copy = remote(psend, precv, core_send.at[0], core_recv.at[0], core_dev)
    pair_copy.start()
    pown[...] = dot_rows(attn[:, s].reshape(heads * share, inner), wo_ref[...]).reshape(
        heads, share, depth
    )
    pair_copy.wait_recv()
    pown[...] = pown[...] + precv[...].reshape(heads, share, depth).astype(f32)
    zsend[...] = pown[...].astype(bf16)
    order = sorted(range(1, heads), key=lambda j: -min(j, heads - j))
    z_copies = {}
    for j in order:
        z_copies[j] = remote(
            zsend.at[lax.rem(h + j, heads)],
            zrecv.at[j - 1],
            z_send.at[j - 1],
            z_recv.at[j - 1],
            z_devs[j - 1],
        )
        z_copies[j].start()
    sent = [pair_copy] + list(z_copies.values())

    slots = 2 * heads * cap
    slot = lax.broadcasted_iota(jnp.int32, (slots, share), 0)
    named = jnp.zeros((slots, share), f32)
    routed = jnp.zeros((slots, share), f32)
    for k in range(ids_ref.shape[0]):
        hit = ids_ref[k : k + 1, :] == slot // cap
        named = named + jnp.where(hit, 1.0, 0.0)
        routed = routed + jnp.where(hit, rw_ref[k : k + 1, :], 0.0)
    earlier = lax.broadcasted_iota(jnp.int32, (share, share), 0) < lax.broadcasted_iota(
        jnp.int32, (share, share), 1
    )
    rank = jnp.dot(
        named.astype(bf16), jnp.where(earlier, 1.0, 0.0).astype(bf16), preferred_element_type=f32
    )
    rank_here = jnp.where(rank == (slot % cap).astype(f32), 1.0, 0.0)
    pick = (named * rank_here).astype(bf16)
    mix = (routed * rank_here).T
    mix_coarse = mix.astype(bf16)
    mix_fine = (mix - mix_coarse.astype(f32)).astype(bf16)

    gathered = res_ref[...].astype(f32) + pown[h]
    for j in range(1, heads):
        z_copies[j].wait_recv()
        gathered = gathered + zrecv[j - 1].astype(f32)
    residual = gathered.astype(bf16)
    resid[...] = residual
    wide = residual.astype(f32)
    mean_square = jnp.mean(wide * wide, axis=-1, keepdims=True)
    normed = (wide * lax.rsqrt(mean_square + EPSILON) * gain_ref[...][None, :]).astype(bf16)
    disp[...] = (
        jnp.dot(pick, normed, preferred_element_type=f32)
        .astype(bf16)
        .reshape(heads, 2, cap, depth)
    )
    zin[h] = disp[h]

    near_first = order[::-1]
    line_in, to_core, across = {}, {}, {}
    for j in near_first:
        sem = heads - 2 + j
        line_in[j] = remote(
            disp.at[lax.rem(h + j, heads)],
            zin.at[h],
            z_send.at[sem],
            z_recv.at[sem],
            z_devs[j - 1],
        )
        line_in[j].start()

    def cross(j, core):
        block = xin.at[r, lax.rem(h - j + heads, heads), core]
        sem = 2 * j + (0 if core is s else 1)
        across[sem] = remote(block, block, x_send.at[sem], x_recv.at[sem], x_dev)
        across[sem].start()

    for j in [0] + near_first:
        if j:
            line_in[j].wait_recv()
        origin = lax.rem(h - j + heads, heads)
        to_core[j] = remote(
            zin.at[origin, 1 - s],
            xin.at[r, origin, s],
            core_send.at[1 + j],
            core_recv.at[1 + j],
            core_dev,
        )
        to_core[j].start()
        xin[r, origin, s] = zin[origin, s]
        cross(j, s)
        to_core[j].wait_recv()
        cross(j, 1 - s)
    for copy in across.values():
        copy.wait_recv()
    sent += list(line_in.values()) + list(to_core.values()) + list(across.values())

    rows_in = 4 * heads * cap
    weight_copies[0].wait()
    weight_copies[1].wait()

    def hidden_tile(tile):
        gate_out = dot_rows(xin[...].reshape(rows_in, depth), wg[tile, :])
        up_out = dot_rows(xin[...].reshape(rows_in, depth), wu[tile, :])
        act[:, tile] = (gate_out * jax.nn.sigmoid(1.702 * gate_out) * (up_out + 1.0)).astype(bf16)

    hidden = wg.shape[0]
    full = hidden // 512

    @pl.loop(0, full)
    def _(i):
        hidden_tile(pl.ds(pl.multiple_of(i * 512, 512), 512))

    if hidden % 512:
        hidden_tile(pl.ds(full * 512, hidden % 512))
    weight_copies[2].wait()

    count = len(chunks)
    per = len(chunk_refs) // count
    base_core, base_x, base_z = 1 + heads, 2 * heads, 2 * (heads - 1)
    x_copies, core_copies, line_copies = {}, {}, {}

    def multiply(c):
        cown, xsend, xrecv, to_other, back_send, back_recv = chunk_refs[c * per : (c + 1) * per]
        start, width = chunks[c]
        cown[...] = jnp.dot(
            act[...], wd[:, start : start + width], preferred_element_type=f32
        ).reshape(2, heads, 2, cap, width)
        xsend[...] = cown[1 - r].astype(bf16)
        x_copies[c] = remote(xsend, xrecv, x_send.at[base_x + c], x_recv.at[base_x + c], x_dev)
        x_copies[c].start()

    def over_req(c):
        cown, xsend, xrecv, to_other, back_send, back_recv = chunk_refs[c * per : (c + 1) * per]
        x_copies[c].wait_recv()
        to_other[...] = (cown[r].astype(bf16).astype(f32) + xrecv[...].astype(f32)).astype(bf16)
        core_copies[c] = remote(
            to_other.at[:, 1 - s],
            back_send.at[:, s],
            core_send.at[base_core + c],
            core_recv.at[base_core + c],
            core_dev,
        )
        core_copies[c].start()
        back_send[:, s] = to_other[:, s]

    def along_line(c):
        cown, xsend, xrecv, to_other, back_send, back_recv = chunk_refs[c * per : (c + 1) * per]
        core_copies[c].wait_recv()
        line_copies[c] = {}
        for j in order:
            sem = base_z + c * (heads - 1) + j - 1
            line_copies[c][j] = remote(
                back_send.at[lax.rem(h + j, heads)],
                back_recv.at[h],
                z_send.at[sem],
                z_recv.at[sem],
                z_devs[j - 1],
            )
            line_copies[c][j].start()
        back_recv[h] = back_send[h]

    def at_rows(c):
        cown, xsend, xrecv, to_other, back_send, back_recv = chunk_refs[c * per : (c + 1) * per]
        start, width = chunks[c]
        for copy in line_copies[c].values():
            copy.wait_recv()
        outs = back_recv[...].reshape(slots, width)
        total = jnp.dot(mix_coarse, outs, preferred_element_type=f32)
        total = total + jnp.dot(mix_fine, outs, preferred_element_type=f32)
        total = total + resid[:, start : start + width].astype(f32)
        out_ref[:, start : start + width] = total.astype(bf16)

    for c in range(count):
        multiply(c)
    for step in range(count + 1):
        for lag, stage in enumerate((over_req, along_line)):
            if 0 <= step - lag < count:
                stage(step - lag)
    for c in range(count):
        at_rows(c)
    sent += list(x_copies.values()) + list(core_copies.values())
    for copies in line_copies.values():
        sent += list(copies.values())
    for copy in sent:
        copy.wait_send()


def fused_on_device(
    queries,
    cache_pool,
    lengths,
    block_table,
    out_proj,
    residual_in,
    norm_gain,
    expert_ids,
    route_weight,
    gate_weight,
    up_weight,
    down_weight,
):
    bf16, f32 = jnp.bfloat16, jnp.float32
    heads = lax.axis_size("head")
    share, depth = residual_in.shape
    inner = queries.shape[1]
    hidden = gate_weight.shape[2]
    cap = share * TOP // (heads * 2)
    tokens = cache_pool.shape[0] * cache_pool.shape[1]
    kv = lax.dynamic_index_in_dim(cache_pool, lax.axis_index("sec"), axis=2, keepdims=False)
    kv = kv.reshape(tokens, cache_pool.shape[3])
    chunks = lane_chunks(depth, CHUNK)
    count = len(chunks)
    vmem = pltpu.VMEM
    scratch = [
        vmem((hidden, depth), bf16),
        vmem((hidden, depth), bf16),
        vmem((hidden, depth), bf16),
        vmem((heads, 2, share, inner), bf16),
        vmem((heads * share, depth), bf16),
        vmem((heads * share, depth), bf16),
        vmem((heads, share, depth), f32),
        vmem((heads, share, depth), bf16),
        vmem((heads - 1, share, depth), bf16),
        vmem((share, depth), bf16),
        vmem((heads, 2, cap, depth), bf16),
        vmem((heads, 2, cap, depth), bf16),
        vmem((2, heads, 2, cap, depth), bf16),
        vmem((4 * heads * cap, hidden), bf16),
        pltpu.SemaphoreType.DMA((3,)),
        pltpu.SemaphoreType.DMA((1 + heads + count,)),
        pltpu.SemaphoreType.DMA((1 + heads + count,)),
        pltpu.SemaphoreType.DMA((2 * heads + count,)),
        pltpu.SemaphoreType.DMA((2 * heads + count,)),
        pltpu.SemaphoreType.DMA(((heads - 1) * (2 + count),)),
        pltpu.SemaphoreType.DMA(((heads - 1) * (2 + count),)),
    ]
    for start, width in chunks:
        scratch += [
            vmem((2, heads, 2, cap, width), f32),
            vmem((heads, 2, cap, width), bf16),
            vmem((heads, 2, cap, width), bf16),
            vmem((heads, 2, cap, width), bf16),
            vmem((heads, 2, cap, width), bf16),
            vmem((heads, 2, cap, width), bf16),
        ]
    in_vmem = pl.BlockSpec(memory_space=pltpu.VMEM)
    in_smem = pl.BlockSpec(memory_space=pltpu.SMEM)
    in_place = pl.BlockSpec(memory_space=pl.ANY)
    return pl.pallas_call(
        functools.partial(layer_kernel, chunks),
        out_shape=jax.ShapeDtypeStruct((share, depth), bf16),
        in_specs=[in_vmem, in_vmem, in_smem, in_smem] + [in_vmem] * 5 + [in_place] * 3,
        out_specs=in_vmem,
        scratch_shapes=scratch,
        compiler_params=pltpu.CompilerParams(
            collective_id=0, has_side_effects=True, vmem_limit_bytes=58 << 20
        ),
    )(
        queries,
        kv,
        lengths,
        block_table,
        out_proj.T,
        residual_in,
        norm_gain,
        expert_ids.T,
        route_weight.T,
        jnp.swapaxes(gate_weight, 1, 2),
        jnp.swapaxes(up_weight, 1, 2),
        down_weight,
    )


def solution(mesh):
    sizes = dict(mesh.shape)
    fused = sizes["req"] == 2 and sizes["sec"] == 2 and sizes["head"] == 4
    return jax.shard_map(
        fused_on_device if fused else on_device,
        mesh=mesh,
        in_specs=(
            P(("groups", "req"), ("head", "sec")),
            P(("groups", "req"), None, "head", None),
            P(("groups", "req")),
            P(("groups", "req"), None),
            P(("head", "sec"), None),
            P(("groups", "req", "head", "sec"), None),
            P(),
            P(("groups", "req", "head", "sec"), None),
            P(("groups", "req", "head", "sec"), None),
            P(("head", "sec"), None, "req"),
            P(("head", "sec"), None, "req"),
            P(("head", "sec"), "req", None),
        ),
        out_specs=P(("groups", "req", "head", "sec"), None),
        check_vma=False,
    )
```
